32 devices in a mesh: group: 2 (over x), tensor: 8 (over z, y), dp: 2 (over core).
Axes of the slice: x: 2, y: 2, z: 4, core: 2. Of those that a mesh axis runs over, the one named last changes fastest.
Arguments:
- features: bfloat16 [512, 8192], P(('group', 'dp'), 'tensor'), parts along dimension 0, may hold values from -64 to 64
- cotangent: bfloat16 [512, 8192], P(('group', 'dp'), 'tensor'), parts along dimension 0, may hold values from -64 to 64
- token_tenant: int32 [512], P(('group', 'dp')), parts along dimension 0, may hold values from 0 to 15
- owner_device: int32 [32], P('group'), parts along dimension 0, may hold values from 0 to 15, each once
- frozen_weight: bfloat16 [8192, 8192], P('tensor'), may hold values from -0.09375 to 0.09375
- adapter_down: bfloat16 [32, 16, 8192], P('group', None, 'tensor'), parts along dimension 0, may hold values from -0.0625 to 0.0625
- adapter_up: bfloat16 [32, 16, 8192], P('group', None, 'tensor'), parts along dimension 0, may hold values from -0.29882812 to 0.29882812
- momentum_down: float32 [32, 16, 8192], P(('group', 'tensor', 'dp')), parts along dimension 0, may hold values from -12 to 12
- momentum_up: float32 [32, 16, 8192], P(('group', 'tensor', 'dp')), parts along dimension 0, may hold values from -3 to 3
- variance_down: float32 [32, 16, 8192], P(('group', 'tensor', 'dp')), parts along dimension 0, may hold values from 0.3 to 3
- variance_up: float32 [32, 16, 8192], P(('group', 'tensor', 'dp')), parts along dimension 0, may hold values from 0.02 to 0.2
Outputs:
- projected: bfloat16 [512, 8192], P(('group', 'dp'), 'tensor'), parts along dimension 0
- updated_down: bfloat16 [32, 16, 8192], P('group', None, 'tensor'), parts along dimension 0
- updated_up: bfloat16 [32, 16, 8192], P('group', None, 'tensor'), parts along dimension 0
- mean_down: float32 [32, 16, 8192], P(('group', 'tensor', 'dp')), parts along dimension 0
- mean_up: float32 [32, 16, 8192], P(('group', 'tensor', 'dp')), parts along dimension 0
- power_down: float32 [32, 16, 8192], P(('group', 'tensor', 'dp')), parts along dimension 0
- power_up: float32 [32, 16, 8192], P(('group', 'tensor', 'dp')), parts along dimension 0
The draws below stay inside these ranges and needn't reach their ends.
There are 2 independent parts, one for each index of `group`. The reference program is written for one: setup_inputs(seed, part) draws one part's arguments, and reference() takes and returns one part's arrays. A program takes and returns all parts, laid end to end along the dimension named above; an argument that names none is the same for every part. Nothing has to cross between parts.
Inputs may be any that keep to these rules, and one draw needn't show every extreme that they name: Tenant t belongs to the device whose index along tensor+dp (dp fastest) is owner_device[t]; every index appears once.
All inputs are finite; a program needn't handle non-finite values.
Results may differ from the reference program's by a relative error of at most 0.0014.
The reference program's roundings to bfloat16 on the way count: a program that leaves them out, or rounds other values in their place, can miss the bound.
Values sent between devices are 32-bit elements; how exact they have to be, the bound alone decides.
A program may use at most 128 MiB of HBM per device.

```python
import math
import jax
import jax.numpy as jnp
import numpy as np
from jax import lax

D = 8192
RANK = 16
TEN = 16
TOKENS = 256


def rough_rows(key, height, breadth):
    subkeys = jax.random.split(key, 3)
    position = jnp.arange(breadth, dtype=jnp.float32) / max(breadth - 1, 1)
    rough_noise = jnp.clip(jax.random.normal(subkeys[0], (height, breadth), jnp.float32), -4.0, 4.0)
    column_trend = jnp.exp(jnp.log(3.0) * position) / 1.7
    row_scale = jnp.exp(jax.random.uniform(subkeys[1], (height, 1), jnp.float32, jnp.log(0.3), jnp.log(3.0)))
    col_scale = column_trend * jnp.exp(jax.random.uniform(subkeys[2], (breadth,), jnp.float32, jnp.log(0.3), jnp.log(3.0)))
    return jnp.clip(rough_noise * row_scale * col_scale[None, :], -64.0, 64.0)


def draw_features(key, part):
    return rough_rows(jax.random.fold_in(key, 11), TOKENS, D).astype(jnp.bfloat16)


def draw_cotangent(key, part):
    return rough_rows(jax.random.fold_in(key, 23), TOKENS, D).astype(jnp.bfloat16)


def set_ends(drawn, stream_key, least, top_value):
    place = [jax.random.randint(jax.random.fold_in(stream_key, axis), (), 0, length) for axis, length in enumerate(drawn.shape)]
    longest = drawn.shape.index(max(drawn.shape))
    neighbour = place[:longest] + [(place[longest] + 1) % drawn.shape[longest]] + place[longest + 1:]
    return drawn.at[tuple(place)].set(least).at[tuple(neighbour)].set(top_value)


def spiked(array, rng, source, target, shards_of, factor):
    def block_of(axis_at):
        return (jnp.arange(array.shape[axis_at]) // (array.shape[axis_at] // shards_of)).reshape((-1,) + (1,) * (array.ndim - 1 - axis_at))

    one_side = jax.random.permutation(rng, shards_of)[block_of(target)]
    other_side = (block_of(target) + shards_of // 2) % shards_of
    return jnp.where((block_of(source) == one_side) | (block_of(source) == other_side), factor * array, array)


def block_levels(key, extent, shards, smallest, largest):
    loudness = 1.0
    for dim, blocks in shards:
        draws = jax.random.uniform(jax.random.fold_in(jax.random.fold_in(key, 6), dim), (blocks,), jnp.float32, smallest / len(shards), largest / len(shards))
        loudness = loudness * jnp.repeat(jnp.exp(draws), extent[dim] // blocks).reshape((-1,) + (1,) * (len(extent) - 1 - dim))
    return loudness


def rank_bounds(number_of, skew):
    loads = [(1 << 20) // math.isqrt(rank ** skew) + 1 for rank in range(1, number_of + 1)]
    scale = 1 + sum(loads) // (1 << 30)
    return np.cumsum(np.array([max(1, weight // scale) for weight in loads]))


def ranked_ids(own_key, shape, count, slope):
    table = rank_bounds(count, slope)
    lot = jax.random.randint(jax.random.fold_in(own_key, 1), shape, 0, int(table[count - 1]))
    grade = jnp.searchsorted(jnp.asarray(table, jnp.int32), lot, side="right")
    return jax.random.permutation(jax.random.fold_in(own_key, 2), count)[grade].astype(jnp.int32)


def scatter_about(stream_key, extent, deviation, bound, cuts=(), held_as=jnp.bfloat16):
    loudness = block_levels(stream_key, extent, cuts, -0.22, 0.18) if cuts else 1.0
    array = jax.random.normal(stream_key, extent, jnp.float32) * deviation * loudness
    return jnp.minimum(jnp.maximum(array, -bound), bound).astype(held_as)


def noise_with(rng, dims, scale, most, pieces, heavy, kind=jnp.bfloat16):
    drawn = scale * jax.random.normal(rng, dims, jnp.float32)
    if pieces:
        drawn = drawn * block_levels(rng, dims, pieces, -0.22, 0.18)
    return jnp.clip(spiked(drawn, jax.random.fold_in(rng, 3), *heavy), -most, most).astype(kind)


def setup_inputs(seed: int = 0, part: int = 0) -> dict:
    splits = jax.random.split(jax.random.key(seed), 12)
    own_keys = jax.random.split(jax.random.fold_in(splits[11], part), 12)
    features = draw_features(jax.random.fold_in(jax.random.fold_in(splits[11], part), 71), part)
    cotangent = draw_cotangent(jax.random.fold_in(jax.random.fold_in(splits[11], part), 71), part)
    token_tenant = set_ends(ranked_ids(own_keys[2], (TOKENS,), TEN, 2), jax.random.fold_in(own_keys[2], 3), 0, TEN - 1).astype(jnp.int32)
    owner_device = jax.random.permutation(own_keys[3], TEN).astype(jnp.int32)
    frozen_weight = noise_with(splits[4], (D, D), D ** -0.5, 0.09375, ((0, 8),), (0, 1, 8, 2.0))
    adapter_down = scatter_about(own_keys[5], (TEN, RANK, D), D ** -0.5, 0.0625, ((2, 8),))
    adapter_up = scatter_about(own_keys[6], (TEN, RANK, D), 0.05, 0.29882812, ((2, 8),))
    momentum_down = scatter_about(own_keys[7], (TEN, RANK, D), 2.0, 12.0, ((0, 16),), jnp.float32)
    momentum_up = scatter_about(own_keys[8], (TEN, RANK, D), 0.5, 3.0, ((0, 16),), jnp.float32)
    variance_down = jnp.clip(jnp.exp(math.log(3.0) - 2.3025851 * jax.random.uniform(own_keys[9], (TEN, RANK, D), jnp.float32) ** block_levels(own_keys[9], (TEN, RANK, D), ((0, 16),), -0.2, 0.2)), 0.3, 3.0)
    variance_up = jnp.clip(jnp.exp(math.log(0.2) - 2.3025851 * jax.random.uniform(own_keys[10], (TEN, RANK, D), jnp.float32) ** block_levels(own_keys[10], (TEN, RANK, D), ((0, 16),), -0.2, 0.2)), 0.02, 0.2)
    return dict(features=features, cotangent=cotangent, token_tenant=token_tenant, owner_device=owner_device, frozen_weight=frozen_weight, adapter_down=adapter_down, adapter_up=adapter_up, momentum_down=momentum_down, momentum_up=momentum_up, variance_down=variance_down, variance_up=variance_up)


adapter_scale = 2.0
clip_norm = 12000.0
learn_rate = 0.004
beta_one = 0.9
beta_two = 0.999
adam_eps = 1e-08
correct_one = 1.0 - beta_one ** 20
correct_two = 1.0 - beta_two ** 20

def tenant_mask(token_tenant, tenants, lowrank):
    columns = lax.broadcasted_iota(jnp.int32, (1, tenants * lowrank), 1) // lowrank
    return token_tenant[:, None] == columns

def rank_fold(tenants, lowrank):
    row_index = lax.broadcasted_iota(jnp.int32, (tenants * lowrank, lowrank), 0) % lowrank
    col_index = lax.broadcasted_iota(jnp.int32, (tenants * lowrank, lowrank), 1)
    return (row_index == col_index).astype(jnp.float32)

def select_rank(scores, token_mask, folding):
    picked = jnp.where(token_mask, scores, jnp.zeros_like(scores))
    return jnp.dot(picked, folding, precision=lax.Precision.HIGHEST, preferred_element_type=jnp.float32)

def spread_rank(values, token_mask, tenants):
    scaled = (adapter_scale * values).astype(jnp.bfloat16)
    tiled_rank = jnp.tile(scaled, (1, tenants))
    return jnp.where(token_mask, tiled_rank, jnp.zeros_like(tiled_rank))

def owner_order(owner_device):
    total = owner_device.shape[0]
    slot_index = lax.broadcasted_iota(jnp.int32, (total, total), 0)
    tenant_index = lax.broadcasted_iota(jnp.int32, (total, total), 1)
    return lax.optimization_barrier(jnp.sum(jnp.where(owner_device[None, :] == slot_index, tenant_index, 0), axis=1)).astype(jnp.int32)

def adam_step(gradient, factor, moment, square):
    clipped = gradient * factor
    moment_next = beta_one * moment + (1.0 - beta_one) * clipped
    square_next = beta_two * square + (1.0 - beta_two) * clipped * clipped
    change = learn_rate * (moment_next / correct_one) / (jnp.sqrt(square_next / correct_two) + adam_eps)
    return (moment_next, square_next, change)

def reference(features, cotangent, token_tenant, owner_device, frozen_weight, adapter_down, adapter_up, momentum_down, momentum_up, variance_down, variance_up):
    tenants, lowrank, width = adapter_down.shape
    token_mask = tenant_mask(token_tenant, tenants, lowrank)
    folding = rank_fold(tenants, lowrank)
    down_flat = adapter_down.reshape(tenants * lowrank, width)
    up_flattened = adapter_up.reshape(tenants * lowrank, width)
    contract = (((1,), (1,)), ((), ()))
    down_sum = select_rank(lax.dot_general(features, down_flat, contract, preferred_element_type=jnp.float32), token_mask, folding)
    up_sum = select_rank(lax.dot_general(cotangent, up_flattened, contract, preferred_element_type=jnp.float32), token_mask, folding)
    frozen_result = jnp.dot(features, frozen_weight, preferred_element_type=jnp.float32)
    down_scattered = spread_rank(down_sum, token_mask, tenants)
    up_scattered = spread_rank(up_sum, token_mask, tenants)
    adapter_result = jnp.dot(down_scattered, up_flattened, preferred_element_type=jnp.float32)
    projected = (frozen_result + adapter_result).astype(jnp.bfloat16)
    outer_product = (((0,), (0,)), ((), ()))
    down_gradient = lax.dot_general(up_scattered, features, outer_product, preferred_element_type=jnp.float32)
    up_gradient = lax.dot_general(down_scattered, cotangent, outer_product, preferred_element_type=jnp.float32)
    down_gradient = down_gradient.reshape(tenants, lowrank, width)
    up_gradient = up_gradient.reshape(tenants, lowrank, width)
    slot_tenant = owner_order(owner_device)
    own_down = jnp.take(down_gradient, slot_tenant, axis=0)
    own_up = jnp.take(up_gradient, slot_tenant, axis=0)
    squares = lax.optimization_barrier(jnp.sum(own_down * own_down, axis=(1, 2))) + lax.optimization_barrier(jnp.sum(own_up * own_up, axis=(1, 2)))
    factor = (clip_norm / jnp.maximum(jnp.sqrt(squares), clip_norm))[:, None, None]
    mean_down, power_down, change_down = adam_step(own_down, factor, momentum_down, variance_down)
    mean_up, power_up, change_up = adam_step(own_up, factor, momentum_up, variance_up)
    back_down = jnp.take(change_down, owner_device, axis=0)
    back_up = jnp.take(change_up, owner_device, axis=0)
    updated_down = (adapter_down.astype(jnp.float32) - back_down).astype(jnp.bfloat16)
    updated_up = (adapter_up.astype(jnp.float32) - back_up).astype(jnp.bfloat16)
    return (projected, updated_down, updated_up, mean_down, mean_up, power_down, power_up)
```

```python
import functools

import jax
import jax.numpy as jnp
from jax import lax
from jax.experimental import pallas as pl
from jax.experimental.pallas import tpu as pltpu
from jax.sharding import PartitionSpec as P

MESH = pl.DeviceIdType.MESH

adapter_scale = 2.0
clip_norm = 12000.0
learn_rate = 0.004
beta_one = 0.9
beta_two = 0.999
adam_eps = 1e-08
correct_one = 1.0 - beta_one**20
correct_two = 1.0 - beta_two**20

CHUNKS = 4
EARLY = 2


def adam_step(gradient, factor, moment, square):
    clipped = gradient * factor
    moment_next = beta_one * moment + (1.0 - beta_one) * clipped
    square_next = beta_two * square + (1.0 - beta_two) * clipped * clipped
    change = (
        learn_rate * (moment_next / correct_one) / (jnp.sqrt(square_next / correct_two) + adam_eps)
    )
    return (moment_next, square_next, change)


def block_order(line, zi):
    low = zi < line // 2
    near = jnp.where(low, zi, line - 1 - zi)
    order = []
    for k in range(line - 1):
        far_first = line - 1 - (k // 2 if k % 2 == 0 else k // 2)
        paired = far_first if k % 2 == 0 else k // 2
        alone = line - 1 - (k - near)
        place = jnp.where(k < 2 * near, paired, alone)
        order.append(jnp.where(low, place, line - 1 - place))
    order.append(zi)
    return order


def kernel(
    n,
    owner_hbm,
    tenant_hbm,
    feat_hbm,
    cot_hbm,
    down_hbm,
    up_hbm,
    weight_ref,
    mom_down_ref,
    mom_up_ref,
    var_down_ref,
    var_up_ref,
    proj_hbm,
    new_down_hbm,
    new_up_hbm,
    mean_down_ref,
    mean_up_ref,
    power_down_ref,
    power_up_ref,
    owner_ref,
    tenant_ref,
    feat_ref,
    cot_ref,
    down_ref,
    up_ref,
    proj_ref,
    new_down_ref,
    new_up_ref,
    wbuf,
    state,
    rpart,
    rbuf,
    gsend,
    grecv,
    summed,
    owned,
    change,
    changes,
    ysend,
    yrecv,
    part,
    going_up,
    going_down,
    adapted,
    isem,
    osem,
    wsem,
    msem,
    rank_s,
    rank_r,
    g_s,
    g_r,
    a_s,
    a_r,
    c_s,
    c_r,
    f_s,
    f_r,
    y_s,
    y_r,
    z_s,
    u_r,
    d_r,
):
    tenants, lowrank, w = down_ref.shape
    tokens, depth = feat_ref.shape
    line = n // 2
    t = lax.axis_index("tensor")
    d = lax.axis_index("dp")
    zi, yi = t // 2, lax.rem(t, 2)
    mate = {"dp": 1 - d}
    pair = {"tensor": zi * 2 + 1 - yi}
    order = block_order(line, zi)
    height = tokens // CHUNKS
    paired = n & (n - 1) == 0

    def peer(o):
        return t ^ (n - o) if paired else lax.rem(t + o, n)

    def giver(o):
        return t ^ (n - o) if paired else lax.rem(t + n - o, n)

    def columns(block):
        return pl.ds(pl.multiple_of(block * w, w), w)

    barrier = pltpu.get_barrier_semaphore()

    @pl.loop(1, n)
    def _(o):
        pl.semaphore_signal(barrier, inc=1, device_id={"tensor": peer(o)}, device_id_type=MESH)

    pl.semaphore_signal(barrier, inc=1, device_id=mate, device_id_type=MESH)

    in_copies = [
        pltpu.make_async_copy(src, dst, isem.at[i])
        for i, (src, dst) in enumerate(
            (
                (tenant_hbm, tenant_ref),
                (feat_hbm, feat_ref),
                (down_hbm, down_ref),
                (cot_hbm, cot_ref),
                (up_hbm, up_ref),
                (owner_hbm, owner_ref),
            )
        )
    ]
    for copy in in_copies:
        copy.start()

    def weight_copy(i, block):
        return pltpu.make_async_copy(
            weight_ref.at[:, columns(block)], wbuf.at[i], wsem.at[i]
        )

    blocks = [z * 2 + 1 - yi for z in order] + [z * 2 + yi for z in order]
    for i, block in enumerate(blocks):
        weight_copy(i, block).start()
    state_copies = [
        pltpu.make_async_copy(ref, state.at[i], msem.at[i])
        for i, ref in enumerate((mom_down_ref, mom_up_ref, var_down_ref, var_up_ref))
    ]
    for copy in state_copies:
        copy.start()

    in_copies[0].wait()
    tenant = tenant_ref[...]
    contract = (((1,), (1,)), ((), ()))
    tenant_row = lax.broadcasted_iota(jnp.int32, (tenants, lowrank, tokens), 0)
    tenant_hit = tenant_row == tenant[None]

    def rank_part(adapter, rows):
        scores = lax.dot_general(
            adapter[...].reshape(tenants * lowrank, w),
            rows[...],
            contract,
            preferred_element_type=jnp.float32,
        ).reshape(tenants, lowrank, tokens)
        return jnp.sum(jnp.where(tenant_hit, scores, 0.0), axis=0)

    in_copies[1].wait()
    in_copies[2].wait()
    rpart[0] = rank_part(down_ref, feat_ref)
    in_copies[3].wait()
    in_copies[4].wait()
    rpart[1] = rank_part(up_ref, cot_ref)
    in_copies[5].wait()

    pl.semaphore_wait(barrier, n)

    def rank_copy(o, source):
        return pltpu.make_async_remote_copy(
            src_ref=rpart,
            dst_ref=rbuf.at[source],
            send_sem=rank_s.at[o],
            recv_sem=rank_r.at[source],
            device_id={"tensor": peer(o)},
            device_id_type=MESH,
        )

    @pl.loop(1, n)
    def _(o):
        rank_copy(o, t).start()

    def rows_of(c):
        return pl.ds(c * height, height)

    def pair_copy(z, c):
        return pltpu.make_async_remote_copy(
            src_ref=ysend.at[z, rows_of(c)],
            dst_ref=yrecv.at[z, rows_of(c)],
            send_sem=y_s.at[z * CHUNKS + c],
            recv_sem=y_r.at[z * CHUNKS + c],
            device_id=pair,
            device_id_type=MESH,
        )

    def pair_start(z):
        for c in range(CHUNKS):
            pair_copy(z, c).start()

    def frozen(i, block):
        weight_copy(i, block).wait()
        return jnp.dot(feat_ref[...], wbuf[i], preferred_element_type=jnp.float32)

    for i, z in enumerate(order):
        ysend[z] = frozen(i, blocks[i])
        if i == 0:
            pair_start(z)

    slot = jnp.zeros_like(tenant)
    slot = lax.fori_loop(
        0, tenants, lambda k, s: jnp.where(tenant == k, owner_ref[k], s), slot
    )

    @pl.loop(1, n)
    def _(o):
        rank_copy(o, giver(o)).wait_recv()

    rbuf[t] = rpart[...]
    total = rbuf[0]
    for source in range(1, n):
        total = total + rbuf[source]
    low = adapter_scale * total
    down_low = low[0].astype(jnp.bfloat16).astype(jnp.float32)
    up_low = low[1].astype(jnp.bfloat16).astype(jnp.float32)

    half_row = lax.broadcasted_iota(jnp.int32, (n, lowrank, tokens), 0) * 2

    def half_grads(side):
        hit = half_row + side == slot[None]

        def one(values, rows):
            spread = jnp.where(hit, values[None], 0.0).reshape(n * lowrank, tokens)
            return jnp.dot(
                spread.astype(jnp.bfloat16), rows[...], preferred_element_type=jnp.float32
            ).reshape(n, lowrank, w)

        return one(up_low, feat_ref), one(down_low, cot_ref)

    def mate_copy(i):
        return pltpu.make_async_remote_copy(
            src_ref=gsend.at[i],
            dst_ref=grecv.at[i],
            send_sem=g_s.at[i],
            recv_sem=g_r.at[i],
            device_id=mate,
            device_id_type=MESH,
        )

    theirs = half_grads(1 - d)
    for i in range(2):
        gsend[i] = theirs[i]
    for i in range(2):
        mate_copy(i).start()
    mine = half_grads(d)
    for i in range(2):
        summed[:, i] = mine[i]
    for i in range(2):
        mate_copy(i).wait_recv()
        summed[:, i] = summed[:, i] + grecv[i]

    def grad_copy(o, source):
        return pltpu.make_async_remote_copy(
            src_ref=summed.at[peer(o)],
            dst_ref=owned.at[source],
            send_sem=a_s.at[o],
            recv_sem=a_r.at[source],
            device_id={"tensor": peer(o)},
            device_id_type=MESH,
        )

    @pl.loop(1, n)
    def _(o):
        grad_copy(o, t).start()

    pair_start(order[1])

    owned[t] = summed[t]

    down_spread = jnp.where(tenant_hit, down_low[None], 0.0).reshape(tenants * lowrank, tokens)
    adapted[...] = jnp.dot(
        jnp.transpose(down_spread).astype(jnp.bfloat16),
        up_ref[...].reshape(tenants * lowrank, w),
        preferred_element_type=jnp.float32,
    )
    for i, z in enumerate(order):
        part[z] = frozen(line + i, blocks[line + i])

    def up_copy(z, c):
        return pltpu.make_async_remote_copy(
            src_ref=part.at[z, rows_of(c)],
            dst_ref=going_up.at[z, rows_of(c)],
            send_sem=z_s.at[z * CHUNKS + c],
            recv_sem=u_r.at[z * CHUNKS + c],
            device_id={"tensor": lax.rem(t + 2, n)},
            device_id_type=MESH,
        )

    def down_copy(z, c):
        return pltpu.make_async_remote_copy(
            src_ref=part.at[z, rows_of(c)],
            dst_ref=going_down.at[z, rows_of(c)],
            send_sem=z_s.at[z * CHUNKS + c],
            recv_sem=d_r.at[z * CHUNKS + c],
            device_id={"tensor": lax.rem(t + n - 2, n)},
            device_id_type=MESH,
        )

    def pair_add(z, c):
        at = rows_of(c)
        pair_copy(z, c).wait_recv()
        part[z, at] = part[z, at] + yrecv[z, at]

    def ends(z, c):
        @pl.when(jnp.logical_and(zi == 0, z > 0))
        def _():
            up_copy(z, c).start()

        @pl.when(jnp.logical_and(zi == line - 1, z < line - 1))
        def _():
            down_copy(z, c).start()

    def middles(z, c):
        at = rows_of(c)

        @pl.when(jnp.logical_and(zi > 0, zi < z))
        def _():
            up_copy(z, c).wait_recv()
            part[z, at] = part[z, at] + going_up[z, at]
            up_copy(z, c).start()

        @pl.when(jnp.logical_and(zi > z, zi < line - 1))
        def _():
            down_copy(z, c).wait_recv()
            part[z, at] = part[z, at] + going_down[z, at]
            down_copy(z, c).start()

    for c in range(CHUNKS):
        pair_add(order[0], c)
        ends(order[0], c)
    for c in range(EARLY):
        middles(order[0], c)

    for copy in state_copies:
        copy.wait()

    @pl.loop(1, n)
    def _(o):
        grad_copy(o, giver(o)).wait_recv()

    def squares_of(k, acc):
        g = owned[k]
        return acc + jnp.sum(g * g, axis=0)

    squares = lax.fori_loop(0, n, squares_of, jnp.zeros((lowrank, w), jnp.float32))
    squares = jnp.sum(squares, axis=(0, 1), keepdims=True)
    factor = clip_norm / jnp.maximum(jnp.sqrt(squares), clip_norm)

    def change_copy(o, source):
        return pltpu.make_async_remote_copy(
            src_ref=change.at[peer(o)],
            dst_ref=changes.at[source * 2 + d],
            send_sem=c_s.at[o],
            recv_sem=c_r.at[source],
            device_id={"tensor": peer(o)},
            device_id_type=MESH,
        )

    def step_piece(k):
        at = columns(k)
        for i in range(2):
            mean, power, moved = adam_step(
                owned[k, i], factor, state[i, 0, :, at], state[2 + i, 0, :, at]
            )
            state[i, 0, :, at] = mean
            state[2 + i, 0, :, at] = power
            change[k, i] = moved

    @pl.loop(1, n)
    def _(o):
        step_piece(peer(o))

        @pl.when(o > 1)
        def _():
            change_copy(o - 1, t).start()

    step_piece(t)
    change_copy(n - 1, t).start()
    changes[t * 2 + d] = change[t]

    for z in order[2:]:
        pair_start(z)

    def forward_copy(source, side):
        at = source * 2 + side
        return pltpu.make_async_remote_copy(
            src_ref=changes.at[at],
            dst_ref=changes.at[at],
            send_sem=f_s.at[source],
            recv_sem=f_r.at[source],
            device_id=mate,
            device_id_type=MESH,
        )

    forward_copy(t, d).start()
    state_outs = [
        pltpu.make_async_copy(state.at[i], ref, msem.at[i])
        for i, ref in enumerate((mean_down_ref, mean_up_ref, power_down_ref, power_up_ref))
    ]
    for copy in state_outs:
        copy.start()

    for c in range(EARLY, CHUNKS):
        middles(order[0], c)
    for c in range(CHUNKS):
        pair_add(order[1], c)
        ends(order[1], c)
        middles(order[1], c)

    @pl.loop(1, n)
    def _(o):
        change_copy(o, giver(o)).wait_recv()
        forward_copy(giver(o), d).start()

    for z in order[2:-1]:
        for c in range(CHUNKS):
            pair_add(z, c)
            ends(z, c)
            middles(z, c)

    @pl.loop(0, n)
    def _(source):
        forward_copy(source, 1 - d).wait_recv()

    @pl.loop(0, tenants)
    def _(k):
        back = changes[owner_ref[k]]
        new_down_ref[k] = (down_ref[k].astype(jnp.float32) - back[0]).astype(jnp.bfloat16)
        new_up_ref[k] = (up_ref[k].astype(jnp.float32) - back[1]).astype(jnp.bfloat16)

    adapter_outs = [
        pltpu.make_async_copy(new_down_ref, new_down_hbm, osem.at[0]),
        pltpu.make_async_copy(new_up_ref, new_up_hbm, osem.at[1]),
    ]
    for copy in adapter_outs:
        copy.start()

    def proj_out(c):
        at = rows_of(c)
        return pltpu.make_async_copy(proj_ref.at[at], proj_hbm.at[at], osem.at[2 + c])

    for c in range(CHUNKS):
        at = rows_of(c)
        pair_add(zi, c)

        @pl.when(zi > 0)
        def _():
            up_copy(zi, c).wait_recv()
            part[zi, at] = part[zi, at] + going_up[zi, at]

        @pl.when(zi < line - 1)
        def _():
            down_copy(zi, c).wait_recv()
            part[zi, at] = part[zi, at] + going_down[zi, at]

        proj_ref[at] = (part[zi, at] + adapted[at]).astype(proj_ref.dtype)
        proj_out(c).start()

    for copy in state_outs + adapter_outs:
        copy.wait()

    @pl.loop(1, n)
    def _(o):
        rank_copy(o, t).wait_send()
        grad_copy(o, t).wait_send()
        change_copy(o, t).wait_send()

    @pl.loop(0, n)
    def _(source):
        forward_copy(source, d).wait_send()

    for i in range(2):
        mate_copy(i).wait_send()
    for z in range(line):
        for c in range(CHUNKS):
            pair_copy(z, c).wait_send()

            @pl.when(zi != z)
            def _():
                up_copy(z, c).wait_send()

    for c in range(CHUNKS):
        proj_out(c).wait()


def hand_out(*refs):
    count = len(refs) // 3
    sources, results, held = refs[:count], refs[count : 2 * count], refs[2 * count : 3 * count]
    sems = refs[-1]
    ins = [pltpu.make_async_copy(sources[i], held[i], sems.at[0, i]) for i in range(count)]
    outs = [pltpu.make_async_copy(held[i], results[i], sems.at[1, i]) for i in range(count)]
    for copy in ins:
        copy.start()
    for i in range(count):
        ins[i].wait()
        outs[i].start()
    for copy in outs:
        copy.wait()


def on_device(n, *args):
    (
        features,
        cotangent,
        token_tenant,
        owner_device,
        frozen_weight,
        adapter_down,
        adapter_up,
        momentum_down,
        momentum_up,
        variance_down,
        variance_up,
    ) = args
    tokens, depth = features.shape
    tenants, lowrank, w = adapter_down.shape
    line = n // 2
    f32 = jnp.float32
    bf16 = jnp.bfloat16
    hbm = pl.BlockSpec(memory_space=pl.ANY)
    dma = pltpu.SemaphoreType.DMA
    shape = jax.ShapeDtypeStruct
    results = pl.pallas_call(
        functools.partial(kernel, n),
        out_shape=(
            shape((tokens, w), jnp.bfloat16),
            shape(adapter_down.shape, jnp.bfloat16),
            shape(adapter_up.shape, jnp.bfloat16),
            shape(momentum_down.shape, f32),
            shape(momentum_up.shape, f32),
            shape(variance_down.shape, f32),
            shape(variance_up.shape, f32),
        ),
        in_specs=[hbm] * 11,
        out_specs=[hbm] * 7,
        scratch_shapes=[
            pltpu.SMEM((tenants,), jnp.int32),
            pltpu.VMEM((1, tokens), jnp.int32),
            pltpu.VMEM((tokens, depth), bf16),
            pltpu.VMEM((tokens, w), bf16),
            pltpu.VMEM(adapter_down.shape, bf16),
            pltpu.VMEM(adapter_up.shape, bf16),
            pltpu.VMEM((tokens, w), bf16),
            pltpu.VMEM(adapter_down.shape, bf16),
            pltpu.VMEM(adapter_up.shape, bf16),
            pltpu.VMEM((n, depth, w), jnp.bfloat16),
            pltpu.VMEM((4,) + momentum_down.shape, f32),
            pltpu.VMEM((2, lowrank, tokens), f32),
            pltpu.VMEM((n, 2, lowrank, tokens), f32),
            pltpu.VMEM((2, n, lowrank, w), f32),
            pltpu.VMEM((2, n, lowrank, w), f32),
            pltpu.VMEM((n, 2, lowrank, w), f32),
            pltpu.VMEM((n, 2, lowrank, w), f32),
            pltpu.VMEM((n, 2, lowrank, w), f32),
            pltpu.VMEM((tenants, 2, lowrank, w), f32),
            pltpu.VMEM((line, tokens, w), f32),
            pltpu.VMEM((line, tokens, w), f32),
            pltpu.VMEM((line, tokens, w), f32),
            pltpu.VMEM((line, tokens, w), f32),
            pltpu.VMEM((line, tokens, w), f32),
            pltpu.VMEM((tokens, w), f32),
            dma((6,)),
            dma((2 + CHUNKS,)),
            dma((n,)),
            dma((4,)),
            dma((n,)),
            dma((n,)),
            dma((2,)),
            dma((2,)),
            dma((n,)),
            dma((n,)),
            dma((n,)),
            dma((n,)),
            dma((n,)),
            dma((n,)),
            dma((line * CHUNKS,)),
            dma((line * CHUNKS,)),
            dma((line * CHUNKS,)),
            dma((line * CHUNKS,)),
            dma((line * CHUNKS,)),
        ],
        compiler_params=pltpu.CompilerParams(
            collective_id=0, has_side_effects=True, vmem_limit_bytes=60 * 1024 * 1024
        ),
    )(
        owner_device,
        token_tenant.reshape(1, tokens),
        features,
        cotangent,
        adapter_down,
        adapter_up,
        frozen_weight,
        momentum_down,
        momentum_up,
        variance_down,
        variance_up,
    )
    return pl.pallas_call(
        hand_out,
        out_shape=tuple(shape(r.shape, r.dtype) for r in results),
        in_specs=[hbm] * len(results),
        out_specs=[hbm] * len(results),
        scratch_shapes=[pltpu.VMEM(r.shape, r.dtype) for r in results]
        + [dma((2, len(results)))],
    )(*results)


def solution(mesh):
    in_specs = (
        P(("group", "dp"), "tensor"),
        P(("group", "dp"), "tensor"),
        P(("group", "dp")),
        P("group"),
        P("tensor", None),
        P("group", None, "tensor"),
        P("group", None, "tensor"),
        P(("group", "tensor", "dp"), None, None),
        P(("group", "tensor", "dp"), None, None),
        P(("group", "tensor", "dp"), None, None),
        P(("group", "tensor", "dp"), None, None),
    )
    out_specs = (
        P(("group", "dp"), "tensor"),
        P("group", None, "tensor"),
        P("group", None, "tensor"),
        P(("group", "tensor", "dp"), None, None),
        P(("group", "tensor", "dp"), None, None),
        P(("group", "tensor", "dp"), None, None),
        P(("group", "tensor", "dp"), None, None),
    )
    return jax.shard_map(
        functools.partial(on_device, mesh.shape["tensor"]),
        mesh=mesh,
        in_specs=in_specs,
        out_specs=out_specs,
        check_vma=False,
    )
```

```python
import functools

import jax
import jax.numpy as jnp
from jax import lax
from jax.experimental import pallas as pl
from jax.experimental.pallas import tpu as pltpu
from jax.sharding import PartitionSpec as P

MESH = pl.DeviceIdType.MESH

adapter_scale = 2.0
clip_norm = 12000.0
learn_rate = 0.004
beta_one = 0.9
beta_two = 0.999
adam_eps = 1e-08
correct_one = 1.0 - beta_one**20
correct_two = 1.0 - beta_two**20

CHUNKS = 4
EARLY = 1
INNER = ((1, 0), (1, 1), (2, 0), (2, 1), (1, 2), (2, 2), (1, 3), (2, 3))


def adam_step(gradient, factor, moment, square):
    clipped = gradient * factor
    moment_next = beta_one * moment + (1.0 - beta_one) * clipped
    square_next = beta_two * square + (1.0 - beta_two) * clipped * clipped
    change = (
        learn_rate * (moment_next / correct_one) / (jnp.sqrt(square_next / correct_two) + adam_eps)
    )
    return (moment_next, square_next, change)


def block_order(line, zi):
    low = zi < line // 2
    near = jnp.where(low, zi, line - 1 - zi)
    order = []
    for k in range(line - 1):
        far_first = line - 1 - (k // 2 if k % 2 == 0 else k // 2)
        paired = far_first if k % 2 == 0 else k // 2
        alone = line - 1 - (k - near)
        place = jnp.where(k < 2 * near, paired, alone)
        order.append(jnp.where(low, place, line - 1 - place))
    order.append(zi)
    return order


def kernel(
    n,
    owner_hbm,
    tenant_hbm,
    feat_hbm,
    cot_hbm,
    down_hbm,
    up_hbm,
    weight_ref,
    mom_down_ref,
    mom_up_ref,
    var_down_ref,
    var_up_ref,
    proj_hbm,
    new_down_hbm,
    new_up_hbm,
    mean_down_ref,
    mean_up_ref,
    power_down_ref,
    power_up_ref,
    owner_ref,
    tenant_ref,
    feat_ref,
    cot_ref,
    down_ref,
    up_ref,
    proj_ref,
    new_down_ref,
    new_up_ref,
    wbuf,
    state,
    rpart,
    rbuf,
    gsend,
    grecv,
    summed,
    owned,
    change,
    changes,
    ysend,
    yrecv,
    part,
    going_up,
    going_down,
    adapted,
    isem,
    osem,
    wsem,
    msem,
    rank_s,
    rank_r,
    g_s,
    g_r,
    a_s,
    a_r,
    c_s,
    c_r,
    f_s,
    f_r,
    y_s,
    y_r,
    z_s,
    u_r,
    d_r,
):
    tenants, lowrank, w = down_ref.shape
    tokens, depth = feat_ref.shape
    line = n // 2
    t = lax.axis_index("tensor")
    d = lax.axis_index("dp")
    zi, yi = t // 2, lax.rem(t, 2)
    mate = {"dp": 1 - d}
    pair = {"tensor": zi * 2 + 1 - yi}
    order = block_order(line, zi)
    height = tokens // CHUNKS
    paired = n & (n - 1) == 0

    def peer(o):
        return t ^ (n - o) if paired else lax.rem(t + o, n)

    def giver(o):
        return t ^ (n - o) if paired else lax.rem(t + n - o, n)

    def columns(block):
        return pl.ds(pl.multiple_of(block * w, w), w)

    barrier = pltpu.get_barrier_semaphore()

    @pl.loop(1, n)
    def _(o):
        pl.semaphore_signal(barrier, inc=1, device_id={"tensor": peer(o)}, device_id_type=MESH)

    pl.semaphore_signal(barrier, inc=1, device_id=mate, device_id_type=MESH)

    in_copies = [
        pltpu.make_async_copy(src, dst, isem.at[i])
        for i, (src, dst) in enumerate(
            (
                (tenant_hbm, tenant_ref),
                (feat_hbm, feat_ref),
                (down_hbm, down_ref),
                (cot_hbm, cot_ref),
                (up_hbm, up_ref),
                (owner_hbm, owner_ref),
            )
        )
    ]
    for copy in in_copies:
        copy.start()

    def weight_copy(i, block):
        return pltpu.make_async_copy(
            weight_ref.at[:, columns(block)], wbuf.at[i], wsem.at[i]
        )

    blocks = [z * 2 + 1 - yi for z in order] + [z * 2 + yi for z in order]
    in_copies[0].wait()
    tenant = tenant_ref[...]
    contract = (((1,), (1,)), ((), ()))
    tenant_row = lax.broadcasted_iota(jnp.int32, (tenants, lowrank, tokens), 0)
    tenant_hit = tenant_row == tenant[None]

    def rank_part(adapter, rows):
        scores = lax.dot_general(
            adapter[...].reshape(tenants * lowrank, w),
            rows[...],
            contract,
            preferred_element_type=jnp.float32,
        ).reshape(tenants, lowrank, tokens)
        return jnp.sum(jnp.where(tenant_hit, scores, 0.0), axis=0)

    in_copies[1].wait()
    in_copies[2].wait()
    rpart[0] = rank_part(down_ref, feat_ref)
    in_copies[3].wait()
    in_copies[4].wait()
    for i, block in enumerate(blocks):
        weight_copy(i, block).start()
    state_copies = [
        pltpu.make_async_copy(ref, state.at[i], msem.at[i])
        for i, ref in enumerate((mom_down_ref, mom_up_ref, var_down_ref, var_up_ref))
    ]
    for copy in state_copies:
        copy.start()
    rpart[1] = rank_part(up_ref, cot_ref)
    in_copies[5].wait()

    pl.semaphore_wait(barrier, n)

    def rank_copy(o, source):
        return pltpu.make_async_remote_copy(
            src_ref=rpart,
            dst_ref=rbuf.at[source],
            send_sem=rank_s.at[0],
            recv_sem=rank_r.at[source],
            device_id={"tensor": peer(o)},
            device_id_type=MESH,
        )

    @pl.loop(1, n)
    def _(o):
        rank_copy(o, t).start()

    def rows_of(c):
        return pl.ds(c * height, height)

    def pair_copy(z, c):
        return pltpu.make_async_remote_copy(
            src_ref=ysend.at[z, rows_of(c)],
            dst_ref=yrecv.at[z, rows_of(c)],
            send_sem=y_s.at[0],
            recv_sem=y_r.at[z * CHUNKS + c],
            device_id=pair,
            device_id_type=MESH,
        )

    def pair_start(z):
        for c in range(CHUNKS):
            pair_copy(z, c).start()

    def frozen(i, block):
        weight_copy(i, block).wait()
        return jnp.dot(feat_ref[...], wbuf[i], preferred_element_type=jnp.float32)

    for i, z in enumerate(order):
        ysend[z] = frozen(i, blocks[i])
        if i == 0:
            pair_start(z)

    slot = jnp.zeros_like(tenant)
    slot = lax.fori_loop(
        0, tenants, lambda k, s: jnp.where(tenant == k, owner_ref[k], s), slot
    )

    @pl.loop(1, n)
    def _(o):
        rank_copy(o, giver(o)).wait_recv()

    rbuf[t] = rpart[...]
    total = rbuf[0]
    for source in range(1, n):
        total = total + rbuf[source]
    low = adapter_scale * total
    down_low = low[0].astype(jnp.bfloat16).astype(jnp.float32)
    up_low = low[1].astype(jnp.bfloat16).astype(jnp.float32)

    half_row = lax.broadcasted_iota(jnp.int32, (n, lowrank, tokens), 0) * 2

    def half_grads(side, values, rows):
        hit = half_row + side == slot[None]
        spread = jnp.where(hit, values[None], 0.0).reshape(n * lowrank, tokens)
        return jnp.dot(
            spread.astype(jnp.bfloat16), rows[...], preferred_element_type=jnp.float32
        ).reshape(n, lowrank, w)

    def mate_copy(i):
        return pltpu.make_async_remote_copy(
            src_ref=gsend.at[i],
            dst_ref=grecv.at[i],
            send_sem=g_s.at[0],
            recv_sem=g_r.at[i],
            device_id=mate,
            device_id_type=MESH,
        )

    def grad_copy(o, source, side):
        return pltpu.make_async_remote_copy(
            src_ref=summed.at[peer(o), side],
            dst_ref=owned.at[source, side],
            send_sem=a_s.at[0],
            recv_sem=a_r.at[source],
            device_id={"tensor": peer(o)},
            device_id_type=MESH,
        )

    both = pl.ds(0, 2)
    sides = ((up_low, feat_ref), (down_low, cot_ref))
    for i in range(2):
        gsend[i] = half_grads(1 - d, *sides[i])
        mate_copy(i).start()
    for i in range(2):
        summed[:, i] = half_grads(d, *sides[i])
        mate_copy(i).wait_recv()
        summed[:, i] = summed[:, i] + grecv[i]

        @pl.loop(1, n)
        def _(o):
            grad_copy(o, t, i).start()

    pair_start(order[1])

    owned[t] = summed[t]

    down_spread = jnp.where(tenant_hit, down_low[None], 0.0).reshape(tenants * lowrank, tokens)
    adapted[...] = jnp.dot(
        jnp.transpose(down_spread).astype(jnp.bfloat16),
        up_ref[...].reshape(tenants * lowrank, w),
        preferred_element_type=jnp.float32,
    )
    for i, z in enumerate(order):
        part[z] = frozen(line + i, blocks[line + i])

    def up_copy(z, c):
        return pltpu.make_async_remote_copy(
            src_ref=part.at[z, rows_of(c)],
            dst_ref=going_up.at[z, rows_of(c)],
            send_sem=z_s.at[0],
            recv_sem=u_r.at[z * CHUNKS + c],
            device_id={"tensor": lax.rem(t + 2, n)},
            device_id_type=MESH,
        )

    def down_copy(z, c):
        return pltpu.make_async_remote_copy(
            src_ref=part.at[z, rows_of(c)],
            dst_ref=going_down.at[z, rows_of(c)],
            send_sem=z_s.at[0],
            recv_sem=d_r.at[z * CHUNKS + c],
            device_id={"tensor": lax.rem(t + n - 2, n)},
            device_id_type=MESH,
        )

    def pair_add(z, c):
        at = rows_of(c)
        pair_copy(z, c).wait_recv()
        part[z, at] = part[z, at] + yrecv[z, at]

    def ends(z, c):
        @pl.when(jnp.logical_and(zi == 0, z > 0))
        def _():
            up_copy(z, c).start()

        @pl.when(jnp.logical_and(zi == line - 1, z < line - 1))
        def _():
            down_copy(z, c).start()

    def middles(z, c):
        at = rows_of(c)

        @pl.when(jnp.logical_and(zi > 0, zi < z))
        def _():
            up_copy(z, c).wait_recv()
            part[z, at] = part[z, at] + going_up[z, at]
            up_copy(z, c).start()

        @pl.when(jnp.logical_and(zi > z, zi < line - 1))
        def _():
            down_copy(z, c).wait_recv()
            part[z, at] = part[z, at] + going_down[z, at]
            down_copy(z, c).start()

    for c in range(CHUNKS):
        pair_add(order[0], c)
        ends(order[0], c)
    for c in range(EARLY):
        middles(order[0], c)

    for copy in state_copies:
        copy.wait()

    @pl.loop(1, n)
    def _(o):
        grad_copy(o, giver(o), both).wait_recv()

    def squares_of(k, acc):
        g = owned[k]
        return acc + jnp.sum(g * g, axis=0)

    squares = lax.fori_loop(0, n, squares_of, jnp.zeros((lowrank, w), jnp.float32))
    squares = jnp.sum(squares, axis=(0, 1), keepdims=True)
    factor = clip_norm / jnp.maximum(jnp.sqrt(squares), clip_norm)

    def change_copy(o, source):
        return pltpu.make_async_remote_copy(
            src_ref=change.at[peer(o)],
            dst_ref=changes.at[source * 2 + d],
            send_sem=c_s.at[0],
            recv_sem=c_r.at[source],
            device_id={"tensor": peer(o)},
            device_id_type=MESH,
        )

    def step_piece(k):
        at = columns(k)
        for i in range(2):
            mean, power, moved = adam_step(
                owned[k, i], factor, state[i, 0, :, at], state[2 + i, 0, :, at]
            )
            state[i, 0, :, at] = mean
            state[2 + i, 0, :, at] = power
            change[k, i] = moved

    @pl.loop(1, n)
    def _(o):
        step_piece(peer(o))

        @pl.when(o > 1)
        def _():
            change_copy(o - 1, t).start()

    step_piece(t)
    change_copy(n - 1, t).start()
    changes[t * 2 + d] = change[t]

    for z in order[2:]:
        pair_start(z)

    def forward_copy(source, side):
        at = source * 2 + side
        return pltpu.make_async_remote_copy(
            src_ref=changes.at[at],
            dst_ref=changes.at[at],
            send_sem=f_s.at[0],
            recv_sem=f_r.at[source],
            device_id=mate,
            device_id_type=MESH,
        )

    forward_copy(t, d).start()
    state_outs = [
        pltpu.make_async_copy(state.at[i], ref, msem.at[i])
        for i, ref in enumerate((mean_down_ref, mean_up_ref, power_down_ref, power_up_ref))
    ]
    for copy in state_outs:
        copy.start()

    inner = jnp.logical_and(zi > 0, zi < line - 1)

    @pl.when(inner)
    def _():
        for c in range(EARLY, CHUNKS):
            middles(order[0], c)
        for k, c in INNER:
            pair_add(order[k], c)
            middles(order[k], c)

    @pl.when(jnp.logical_not(inner))
    def _():
        for k in (1, 2):
            for c in range(CHUNKS):
                pair_add(order[k], c)
                ends(order[k], c)

    for z in order[3:-1]:
        for c in range(CHUNKS):
            pair_add(z, c)
            ends(z, c)
            middles(z, c)

    @pl.loop(1, n)
    def _(o):
        change_copy(o, giver(o)).wait_recv()
        forward_copy(giver(o), d).start()

    @pl.loop(0, n)
    def _(source):
        forward_copy(source, 1 - d).wait_recv()

    @pl.loop(0, tenants)
    def _(k):
        back = changes[owner_ref[k]]
        new_down_ref[k] = (down_ref[k].astype(jnp.float32) - back[0]).astype(jnp.bfloat16)
        new_up_ref[k] = (up_ref[k].astype(jnp.float32) - back[1]).astype(jnp.bfloat16)

    adapter_outs = [
        pltpu.make_async_copy(new_down_ref, new_down_hbm, osem.at[0]),
        pltpu.make_async_copy(new_up_ref, new_up_hbm, osem.at[1]),
    ]
    for copy in adapter_outs:
        copy.start()

    def proj_out(c):
        at = rows_of(c)
        return pltpu.make_async_copy(proj_ref.at[at], proj_hbm.at[at], osem.at[2 + c])

    for c in range(CHUNKS):
        at = rows_of(c)
        pair_add(zi, c)

        @pl.when(zi > 0)
        def _():
            up_copy(zi, c).wait_recv()
            part[zi, at] = part[zi, at] + going_up[zi, at]

        @pl.when(zi < line - 1)
        def _():
            down_copy(zi, c).wait_recv()
            part[zi, at] = part[zi, at] + going_down[zi, at]

        proj_ref[at] = (part[zi, at] + adapted[at]).astype(proj_ref.dtype)
        proj_out(c).start()

    for copy in state_outs + adapter_outs:
        copy.wait()

    def sent(ref, sem):
        pltpu.make_async_copy(ref, ref, sem).wait()

    sent(rbuf.at[pl.ds(0, n - 1)], rank_s.at[0])
    sent(gsend, g_s.at[0])
    sent(change.at[pl.ds(0, n - 1)], a_s.at[0])
    sent(change.at[pl.ds(0, n - 1)], c_s.at[0])
    sent(changes.at[pl.ds(0, n)], f_s.at[0])
    sent(ysend, y_s.at[0])
    sent(part.at[pl.ds(0, line - 1)], z_s.at[0])
    for c in range(CHUNKS):
        proj_out(c).wait()


def hand_out(*refs):
    count = len(refs) // 2
    sems = refs[-1]
    outs = [pltpu.make_async_copy(refs[i], refs[count + i], sems.at[i]) for i in range(count)]
    for copy in outs:
        copy.start()
    for copy in outs:
        copy.wait()


def on_device(n, *args):
    (
        features,
        cotangent,
        token_tenant,
        owner_device,
        frozen_weight,
        adapter_down,
        adapter_up,
        momentum_down,
        momentum_up,
        variance_down,
        variance_up,
    ) = args
    tokens, depth = features.shape
    tenants, lowrank, w = adapter_down.shape
    line = n // 2
    f32 = jnp.float32
    bf16 = jnp.bfloat16
    hbm = pl.BlockSpec(memory_space=pltpu.HBM)
    anywhere = pl.BlockSpec(memory_space=pl.ANY)
    dma = pltpu.SemaphoreType.DMA
    shape = jax.ShapeDtypeStruct
    results = pl.pallas_call(
        functools.partial(kernel, n),
        out_shape=(
            shape((tokens, w), jnp.bfloat16),
            shape(adapter_down.shape, jnp.bfloat16),
            shape(adapter_up.shape, jnp.bfloat16),
            shape(momentum_down.shape, f32),
            shape(momentum_up.shape, f32),
            shape(variance_down.shape, f32),
            shape(variance_up.shape, f32),
        ),
        in_specs=[hbm] * 11,
        out_specs=[anywhere] * 7,
        scratch_shapes=[
            pltpu.SMEM((tenants,), jnp.int32),
            pltpu.VMEM((1, tokens), jnp.int32),
            pltpu.VMEM((tokens, depth), bf16),
            pltpu.VMEM((tokens, w), bf16),
            pltpu.VMEM(adapter_down.shape, bf16),
            pltpu.VMEM(adapter_up.shape, bf16),
            pltpu.VMEM((tokens, w), bf16),
            pltpu.VMEM(adapter_down.shape, bf16),
            pltpu.VMEM(adapter_up.shape, bf16),
            pltpu.VMEM((n, depth, w), jnp.bfloat16),
            pltpu.VMEM((4,) + momentum_down.shape, f32),
            pltpu.VMEM((2, lowrank, tokens), f32),
            pltpu.VMEM((n, 2, lowrank, tokens), f32),
            pltpu.VMEM((2, n, lowrank, w), f32),
            pltpu.VMEM((2, n, lowrank, w), f32),
            pltpu.VMEM((n, 2, lowrank, w), f32),
            pltpu.VMEM((n, 2, lowrank, w), f32),
            pltpu.VMEM((n, 2, lowrank, w), f32),
            pltpu.VMEM((tenants, 2, lowrank, w), f32),
            pltpu.VMEM((line, tokens, w), f32),
            pltpu.VMEM((line, tokens, w), f32),
            pltpu.VMEM((line, tokens, w), f32),
            pltpu.VMEM((line, tokens, w), f32),
            pltpu.VMEM((line, tokens, w), f32),
            pltpu.VMEM((tokens, w), f32),
            dma((6,)),
            dma((2 + CHUNKS,)),
            dma((n,)),
            dma((4,)),
            dma((1,)),
            dma((n,)),
            dma((1,)),
            dma((2,)),
            dma((1,)),
            dma((n,)),
            dma((1,)),
            dma((n,)),
            dma((1,)),
            dma((n,)),
            dma((1,)),
            dma((line * CHUNKS,)),
            dma((1,)),
            dma((line * CHUNKS,)),
            dma((line * CHUNKS,)),
        ],
        compiler_params=pltpu.CompilerParams(
            collective_id=0, has_side_effects=True, vmem_limit_bytes=48 * 1024 * 1024
        ),
    )(
        *(
            pltpu.with_memory_space_constraint(x, pltpu.HBM)
            for x in (
                owner_device,
                token_tenant.reshape(1, tokens),
                features,
                cotangent,
                adapter_down,
                adapter_up,
                frozen_weight,
                momentum_down,
                momentum_up,
                variance_down,
                variance_up,
            )
        )
    )
    return pl.pallas_call(
        hand_out,
        out_shape=tuple(shape(r.shape, r.dtype) for r in results),
        in_specs=[anywhere] * len(results),
        out_specs=[hbm] * len(results),
        scratch_shapes=[dma((len(results),))],
        compiler_params=pltpu.CompilerParams(vmem_limit_bytes=1024 * 1024),
    )(*results)


def solution(mesh):
    in_specs = (
        P(("group", "dp"), "tensor"),
        P(("group", "dp"), "tensor"),
        P(("group", "dp")),
        P("group"),
        P("tensor", None),
        P("group", None, "tensor"),
        P("group", None, "tensor"),
        P(("group", "tensor", "dp"), None, None),
        P(("group", "tensor", "dp"), None, None),
        P(("group", "tensor", "dp"), None, None),
        P(("group", "tensor", "dp"), None, None),
    )
    out_specs = (
        P(("group", "dp"), "tensor"),
        P("group", None, "tensor"),
        P("group", None, "tensor"),
        P(("group", "tensor", "dp"), None, None),
        P(("group", "tensor", "dp"), None, None),
        P(("group", "tensor", "dp"), None, None),
        P(("group", "tensor", "dp"), None, None),
    )
    return jax.shard_map(
        functools.partial(on_device, mesh.shape["tensor"]),
        mesh=mesh,
        in_specs=in_specs,
        out_specs=out_specs,
        check_vma=False,
    )
```

```python
import functools

import jax
import jax.numpy as jnp
from jax import lax
from jax.experimental import pallas as pl
from jax.experimental.pallas import tpu as pltpu
from jax.sharding import PartitionSpec as P

MESH = pl.DeviceIdType.MESH

adapter_scale = 2.0
clip_norm = 12000.0
learn_rate = 0.004
beta_one = 0.9
beta_two = 0.999
adam_eps = 1e-08
correct_one = 1.0 - beta_one**20
correct_two = 1.0 - beta_two**20

CHUNKS = 4
EARLY = 1
LEND_AT = 3
INNER = ((1, 0), (1, 1), (2, 0), (2, 1), (1, 2), (2, 2), (1, 3), (2, 3))


def adam_step(gradient, factor, moment, square):
    clipped = gradient * factor
    moment_next = beta_one * moment + (1.0 - beta_one) * clipped
    square_next = beta_two * square + (1.0 - beta_two) * clipped * clipped
    change = (
        learn_rate * (moment_next / correct_one) / (jnp.sqrt(square_next / correct_two) + adam_eps)
    )
    return (moment_next, square_next, change)


def block_order(line, zi):
    low = zi < line // 2
    near = jnp.where(low, zi, line - 1 - zi)
    order = []
    for k in range(line - 1):
        far_first = line - 1 - (k // 2 if k % 2 == 0 else k // 2)
        paired = far_first if k % 2 == 0 else k // 2
        alone = line - 1 - (k - near)
        place = jnp.where(k < 2 * near, paired, alone)
        order.append(jnp.where(low, place, line - 1 - place))
    order.append(zi)
    return order


def kernel(
    n,
    owner_hbm,
    tenant_hbm,
    feat_hbm,
    cot_hbm,
    down_hbm,
    up_hbm,
    weight_ref,
    mom_down_ref,
    mom_up_ref,
    var_down_ref,
    var_up_ref,
    proj_hbm,
    new_down_hbm,
    new_up_hbm,
    mean_down_ref,
    mean_up_ref,
    power_down_ref,
    power_up_ref,
    owner_ref,
    tenant_ref,
    mate_tenant,
    rows_ref,
    down_ref,
    up_ref,
    proj_ref,
    new_down_ref,
    new_up_ref,
    wbuf,
    state,
    rpart,
    rbuf,
    raw_out,
    raw_in,
    low_out,
    low_in,
    summed,
    owned,
    change,
    changes,
    ysend,
    yrecv,
    part,
    going_up,
    going_down,
    adapted,
    lent,
    scale_out,
    scale_in,
    isem,
    osem,
    wsem,
    msem,
    rank_s,
    rank_r,
    g_s,
    g_r,
    a_s,
    a_r,
    c_s,
    c_r,
    f_s,
    f_r,
    y_s,
    y_r,
    z_s,
    z_r,
    l_s,
    l_r,
    h_s,
    s_r,
):
    tenants, lowrank, w = down_ref.shape
    tokens = tenant_ref.shape[1]
    feat_ref, cot_ref = (rows_ref.at[i, pl.ds(0, tokens)] for i in range(2))
    line = n // 2
    t = lax.axis_index("tensor")
    d = lax.axis_index("dp")
    zi, yi = t // 2, lax.rem(t, 2)
    mate = {"dp": 1 - d}
    pair = {"tensor": zi * 2 + 1 - yi}
    order = block_order(line, zi)
    height = tokens // CHUNKS
    low_side = zi < line // 2
    lent_to = jnp.where(low_side, t + 2, t - 2)
    lent_way = jnp.where(low_side, 0, 1)
    from_below = jnp.logical_and(zi > 0, zi - 1 < line // 2)
    from_above = jnp.logical_and(zi < line - 1, zi + 1 >= line // 2)
    paired = n & (n - 1) == 0

    def peer(o):
        return t ^ (n - o) if paired else lax.rem(t + o, n)

    def giver(o):
        return t ^ (n - o) if paired else lax.rem(t + n - o, n)

    def columns(block):
        return pl.ds(pl.multiple_of(block * w, w), w)

    def sent(ref, sem):
        pltpu.make_async_copy(ref, ref, sem).wait()

    barrier = pltpu.get_barrier_semaphore()

    in_copies = [
        pltpu.make_async_copy(src, dst, isem.at[i])
        for i, (src, dst) in enumerate(
            (
                (tenant_hbm, tenant_ref),
                (feat_hbm, feat_ref),
                (down_hbm, down_ref),
                (cot_hbm, cot_ref),
                (up_hbm, up_ref),
                (owner_hbm, owner_ref),
            )
        )
    ]
    for copy in in_copies:
        copy.start()

    @pl.loop(1, n)
    def _(o):
        pl.semaphore_signal(barrier, inc=1, device_id={"tensor": peer(o)}, device_id_type=MESH)

    pl.semaphore_signal(barrier, inc=1, device_id=mate, device_id_type=MESH)

    def weight_copy(i, block):
        return pltpu.make_async_copy(
            weight_ref.at[:, columns(block)], wbuf.at[i], wsem.at[i]
        )

    blocks = [z * 2 + 1 - yi for z in order] + [z * 2 + yi for z in order]
    in_copies[0].wait()
    tenant = tenant_ref[...]
    contract = (((1,), (1,)), ((), ()))
    tenant_row = lax.broadcasted_iota(jnp.int32, (tenants, lowrank, tokens), 0)
    tenant_hit = tenant_row == tenant[None]

    def rank_part(adapter, rows):
        scores = lax.dot_general(
            adapter[...].reshape(tenants * lowrank, w),
            rows[...],
            contract,
            preferred_element_type=jnp.float32,
        ).reshape(tenants, lowrank, tokens)
        return jnp.sum(jnp.where(tenant_hit, scores, 0.0), axis=0)

    for copy in in_copies[1:5]:
        copy.wait()
    for i, block in enumerate(blocks):
        weight_copy(i, block).start()
    state_copies = [
        pltpu.make_async_copy(ref, state.at[i], msem.at[0])
        for i, ref in enumerate((mom_down_ref, mom_up_ref, var_down_ref, var_up_ref))
    ]
    for copy in state_copies:
        copy.start()
    down_part = rank_part(down_ref, feat_ref)
    up_part = rank_part(up_ref, cot_ref)
    rpart[0] = down_part
    rpart[1] = up_part
    in_copies[5].wait()

    pl.semaphore_wait(barrier, n)

    def rank_copy(o, source):
        return pltpu.make_async_remote_copy(
            src_ref=rpart,
            dst_ref=rbuf.at[source],
            send_sem=rank_s.at[0],
            recv_sem=rank_r.at[source],
            device_id={"tensor": peer(o)},
            device_id_type=MESH,
        )

    @pl.loop(1, n)
    def _(o):
        rank_copy(o, t).start()

    def mate_copy(source, target, out, arrived):
        return pltpu.make_async_remote_copy(
            src_ref=source,
            dst_ref=target,
            send_sem=g_s.at[out],
            recv_sem=g_r.at[arrived],
            device_id=mate,
            device_id_type=MESH,
        )

    tenant_copy = mate_copy(tenant_ref, mate_tenant, 0, 0)
    raw_copies = [mate_copy(raw_out.at[i], raw_in.at[i], 1, 1 + i) for i in range(2)]
    low_copy = mate_copy(low_out, low_in, 2, 3)
    tenant_copy.start()
    for i, rows in enumerate((feat_ref, cot_ref)):
        raw_out[i] = rows[...].astype(jnp.float32)
        raw_copies[i].start()

    def lent_copy(i):
        return pltpu.make_async_remote_copy(
            src_ref=(mom_down_ref, var_down_ref)[i].at[0, :, columns(lent_to)],
            dst_ref=lent.at[lent_way, i],
            send_sem=l_s.at[0],
            recv_sem=l_r.at[lent_way],
            device_id={"tensor": lent_to},
            device_id_type=MESH,
        )

    def rows_of(c):
        return pl.ds(c * height, height)

    def pair_copy(z, c):
        return pltpu.make_async_remote_copy(
            src_ref=ysend.at[z, rows_of(c)],
            dst_ref=yrecv.at[z, rows_of(c)],
            send_sem=y_s.at[0],
            recv_sem=y_r.at[z * CHUNKS + c],
            device_id=pair,
            device_id_type=MESH,
        )

    def pair_start(z):
        for c in range(CHUNKS):
            pair_copy(z, c).start()

    def frozen(i, block):
        weight_copy(i, block).wait()
        return jnp.dot(feat_ref[...], wbuf[i], preferred_element_type=jnp.float32)

    for i, z in enumerate(order):
        ysend[z] = frozen(i, blocks[i])
        if i == 0:
            pair_start(z)
        if i == LEND_AT:
            for k in range(2):
                lent_copy(k).start()

    tenant_copy.wait_recv()
    tenants_here = (tenant, mate_tenant[...])
    slots = lax.fori_loop(
        0,
        tenants,
        lambda k, found: tuple(
            jnp.where(here == k, owner_ref[k], s) for here, s in zip(tenants_here, found)
        ),
        tuple(jnp.zeros_like(here) for here in tenants_here),
    )
    for i in range(2):
        raw_copies[i].wait_recv()
        rows_ref[i, tokens:] = raw_in[i].astype(jnp.bfloat16)

    @pl.loop(1, n)
    def _(o):
        rank_copy(o, giver(o)).wait_recv()

    rbuf[t] = rpart[...]
    total = rbuf[0]
    for source in range(1, n):
        total = total + rbuf[source]
    low = adapter_scale * total
    down_low = low[0].astype(jnp.bfloat16).astype(jnp.float32)
    up_low = low[1].astype(jnp.bfloat16).astype(jnp.float32)

    low_out[0] = up_low
    low_out[1] = down_low
    low_copy.start()

    half_row = lax.broadcasted_iota(jnp.int32, (n, lowrank, tokens), 0) * 2 + d

    def spread(values, slot):
        picked = jnp.where(half_row == slot[None], values[None], 0.0)
        return picked.reshape(n * lowrank, tokens).astype(jnp.bfloat16)

    def grad_copy(o, source, side):
        return pltpu.make_async_remote_copy(
            src_ref=summed.at[peer(o), side],
            dst_ref=owned.at[source, side],
            send_sem=a_s.at[0],
            recv_sem=a_r.at[source],
            device_id={"tensor": peer(o)},
            device_id_type=MESH,
        )

    both = pl.ds(0, 2)
    own_part = [spread(low, slots[0]) for low in (up_low, down_low)]
    low_copy.wait_recv()
    for i in range(2):
        summed[:, i] = jnp.dot(
            jnp.concatenate([own_part[i], spread(low_in[i], slots[1])], axis=1),
            rows_ref[i],
            preferred_element_type=jnp.float32,
        ).reshape(n, lowrank, w)

        @pl.loop(1, n)
        def _(o):
            grad_copy(o, t, i).start()

    pair_start(order[1])

    owned[t] = summed[t]

    down_spread = jnp.where(tenant_hit, down_low[None], 0.0).reshape(tenants * lowrank, tokens)
    adapted[...] = jnp.dot(
        jnp.transpose(down_spread).astype(jnp.bfloat16),
        up_ref[...].reshape(tenants * lowrank, w),
        preferred_element_type=jnp.float32,
    )
    for i, z in enumerate(order):
        part[z] = frozen(line + i, blocks[line + i])

    def up_copy(z, c):
        return pltpu.make_async_remote_copy(
            src_ref=part.at[z, rows_of(c)],
            dst_ref=going_up.at[z, rows_of(c)],
            send_sem=z_s.at[0],
            recv_sem=z_r.at[z * CHUNKS + c],
            device_id={"tensor": lax.rem(t + 2, n)},
            device_id_type=MESH,
        )

    def down_copy(z, c, last=False):
        slot_at = line if last else z
        return pltpu.make_async_remote_copy(
            src_ref=part.at[z, rows_of(c)],
            dst_ref=going_down.at[z, rows_of(c)],
            send_sem=z_s.at[0],
            recv_sem=z_r.at[slot_at * CHUNKS + c],
            device_id={"tensor": lax.rem(t + n - 2, n)},
            device_id_type=MESH,
        )

    def send_down(z, c):
        @pl.when(z == zi - 1)
        def _():
            down_copy(z, c, True).start()

        @pl.when(z < zi - 1)
        def _():
            down_copy(z, c).start()

    def pair_add(z, c):
        at = rows_of(c)
        pair_copy(z, c).wait_recv()
        part[z, at] = part[z, at] + yrecv[z, at]

    def ends(z, c):
        @pl.when(jnp.logical_and(zi == 0, z > 0))
        def _():
            up_copy(z, c).start()

        @pl.when(jnp.logical_and(zi == line - 1, z < line - 1))
        def _():
            send_down(z, c)

    def middles(z, c):
        at = rows_of(c)

        @pl.when(jnp.logical_and(zi > 0, zi < z))
        def _():
            up_copy(z, c).wait_recv()
            part[z, at] = part[z, at] + going_up[z, at]
            up_copy(z, c).start()

        @pl.when(jnp.logical_and(zi > z, zi < line - 1))
        def _():
            down_copy(z, c).wait_recv()
            part[z, at] = part[z, at] + going_down[z, at]
            send_down(z, c)

    for c in range(CHUNKS):
        pair_add(order[0], c)
        ends(order[0], c)
    for c in range(EARLY):
        middles(order[0], c)

    sent(state, msem.at[0])

    @pl.loop(1, n)
    def _(o):
        grad_copy(o, giver(o), both).wait_recv()

    def squares_of(k, acc):
        g = owned[k]
        return acc + jnp.sum(g * g, axis=0)

    squares = lax.fori_loop(0, n, squares_of, jnp.zeros((lowrank, w), jnp.float32))
    squares = jnp.sum(squares, axis=(0, 1), keepdims=True)
    factor = clip_norm / jnp.maximum(jnp.sqrt(squares), clip_norm)

    def change_copy(o, source):
        return pltpu.make_async_remote_copy(
            src_ref=change.at[peer(o)],
            dst_ref=changes.at[source * 2 + d],
            send_sem=c_s.at[0],
            recv_sem=c_r.at[source],
            device_id={"tensor": peer(o)},
            device_id_type=MESH,
        )

    def half_copy(source):
        return pltpu.make_async_remote_copy(
            src_ref=change.at[lent_to, 1],
            dst_ref=changes.at[source * 2 + d, 1],
            send_sem=h_s.at[0],
            recv_sem=c_r.at[source],
            device_id={"tensor": lent_to},
            device_id_type=MESH,
        )

    scale_copy = pltpu.make_async_remote_copy(
        src_ref=scale_out,
        dst_ref=scale_in.at[lent_way],
        send_sem=h_s.at[1],
        recv_sem=s_r.at[lent_way],
        device_id={"tensor": lent_to},
        device_id_type=MESH,
    )
    scale_out[...] = jnp.broadcast_to(factor, scale_out.shape)
    scale_copy.start()

    def change_start(o):
        @pl.when(peer(o) != lent_to)
        def _():
            change_copy(o, t).start()

        @pl.when(peer(o) == lent_to)
        def _():
            half_copy(t).start()

    def step_piece(k):
        at = columns(k)
        for i in range(2):
            mean, power, moved = adam_step(
                owned[k, i], factor, state[i, 0, :, at], state[2 + i, 0, :, at]
            )
            state[i, 0, :, at] = mean
            state[2 + i, 0, :, at] = power
            change[k, i] = moved

    @pl.loop(1, n)
    def _(o):
        step_piece(peer(o))

        @pl.when(o > 1)
        def _():
            change_start(o - 1)

    step_piece(t)
    change_start(n - 1)
    changes[t * 2 + d] = change[t]

    for z in order[2:]:
        pair_start(z)

    def forward_copy(source, side):
        at = source * 2 + side
        return pltpu.make_async_remote_copy(
            src_ref=changes.at[at],
            dst_ref=changes.at[at],
            send_sem=f_s.at[0],
            recv_sem=f_r.at[source],
            device_id=mate,
            device_id_type=MESH,
        )

    forward_copy(t, d).start()
    state_outs = [
        pltpu.make_async_copy(state.at[i], ref, msem.at[0])
        for i, ref in enumerate((mean_down_ref, mean_up_ref, power_down_ref, power_up_ref))
    ]
    for copy in state_outs:
        copy.start()

    inner = jnp.logical_and(zi > 0, zi < line - 1)

    @pl.when(inner)
    def _():
        for c in range(EARLY, CHUNKS):
            middles(order[0], c)
        for k, c in INNER:
            pair_add(order[k], c)
            middles(order[k], c)

    @pl.when(jnp.logical_not(inner))
    def _():
        for k in (1, 2):
            for c in range(CHUNKS):
                pair_add(order[k], c)
                ends(order[k], c)

    for z in order[3:-1]:
        for c in range(CHUNKS):
            pair_add(z, c)
            ends(z, c)
            middles(z, c)

    @pl.loop(1, n)
    def _(o):
        source = giver(o)
        below = jnp.logical_and(from_below, source == t - 2)
        above = jnp.logical_and(from_above, source == t + 2)
        borrowed = jnp.logical_or(below, above)

        @pl.when(jnp.logical_not(borrowed))
        def _():
            change_copy(o, source).wait_recv()

        @pl.when(borrowed)
        def _():
            way = jnp.where(below, 0, 1)
            half_copy(source).wait_recv()
            sent(scale_in.at[way], s_r.at[way])
            sent(lent.at[way], l_r.at[way])
            scale = scale_in[way]
            changes[source * 2 + d, 0] = adam_step(
                summed[source, 0], scale[:1, :1], lent[way, 0], lent[way, 1]
            )[2]

        forward_copy(source, d).start()

    @pl.loop(0, n)
    def _(source):
        forward_copy(source, 1 - d).wait_recv()

    @pl.loop(0, tenants)
    def _(k):
        back = changes[owner_ref[k]]
        new_down_ref[k] = (down_ref[k].astype(jnp.float32) - back[0]).astype(jnp.bfloat16)
        new_up_ref[k] = (up_ref[k].astype(jnp.float32) - back[1]).astype(jnp.bfloat16)

    adapter_outs = [
        pltpu.make_async_copy(new_down_ref, new_down_hbm, osem.at[0]),
        pltpu.make_async_copy(new_up_ref, new_up_hbm, osem.at[1]),
    ]
    for copy in adapter_outs:
        copy.start()

    def proj_out(c):
        at = rows_of(c)
        return pltpu.make_async_copy(proj_ref.at[at], proj_hbm.at[at], osem.at[2])

    for c in range(CHUNKS):
        at = rows_of(c)
        pair_add(zi, c)

        @pl.when(zi > 0)
        def _():
            up_copy(zi, c).wait_recv()
            part[zi, at] = part[zi, at] + going_up[zi, at]

        @pl.when(zi < line - 1)
        def _():
            down_copy(zi, c, True).wait_recv()
            part[zi, at] = part[zi, at] + going_down[zi, at]

        proj_ref[at] = (part[zi, at] + adapted[at]).astype(proj_ref.dtype)
        proj_out(c).start()

    sent(state, msem.at[0])
    for copy in adapter_outs:
        copy.wait()

    sent(rbuf.at[pl.ds(0, n - 1)], rank_s.at[0])
    tenant_copy.wait_send()
    sent(raw_out, g_s.at[1])
    low_copy.wait_send()
    sent(change.at[pl.ds(0, n - 1)], a_s.at[0])
    sent(change.at[pl.ds(0, n - 2)], c_s.at[0])
    sent(change.at[0, 0], h_s.at[0])
    sent(scale_out, h_s.at[1])
    sent(lent.at[0], l_s.at[0])
    sent(changes.at[pl.ds(0, n)], f_s.at[0])
    sent(ysend, y_s.at[0])
    sent(part.at[pl.ds(0, line - 1)], z_s.at[0])
    sent(proj_ref, osem.at[2])


def hand_out(*refs):
    count = len(refs) // 2
    sems = refs[-1]
    outs = [pltpu.make_async_copy(refs[i], refs[count + i], sems.at[i]) for i in range(count)]
    for copy in outs:
        copy.start()
    for copy in outs:
        copy.wait()


def on_device(n, *args):
    (
        features,
        cotangent,
        token_tenant,
        owner_device,
        frozen_weight,
        adapter_down,
        adapter_up,
        momentum_down,
        momentum_up,
        variance_down,
        variance_up,
    ) = args
    tokens, depth = features.shape
    tenants, lowrank, w = adapter_down.shape
    line = n // 2
    f32 = jnp.float32
    bf16 = jnp.bfloat16
    hbm = pl.BlockSpec(memory_space=pltpu.HBM)
    anywhere = pl.BlockSpec(memory_space=pl.ANY)
    dma = pltpu.SemaphoreType.DMA
    shape = jax.ShapeDtypeStruct
    results = pl.pallas_call(
        functools.partial(kernel, n),
        out_shape=(
            shape((tokens, w), jnp.bfloat16),
            shape(adapter_down.shape, jnp.bfloat16),
            shape(adapter_up.shape, jnp.bfloat16),
            shape(momentum_down.shape, f32),
            shape(momentum_up.shape, f32),
            shape(variance_down.shape, f32),
            shape(variance_up.shape, f32),
        ),
        in_specs=[hbm] * 11,
        out_specs=[anywhere] * 7,
        scratch_shapes=[
            pltpu.SMEM((tenants,), jnp.int32),
            pltpu.VMEM((1, tokens), jnp.int32),
            pltpu.VMEM((1, tokens), jnp.int32),
            pltpu.VMEM((2, 2 * tokens, w), bf16),
            pltpu.VMEM(adapter_down.shape, bf16),
            pltpu.VMEM(adapter_up.shape, bf16),
            pltpu.VMEM((tokens, w), bf16),
            pltpu.VMEM(adapter_down.shape, bf16),
            pltpu.VMEM(adapter_up.shape, bf16),
            pltpu.VMEM((n, depth, w), jnp.bfloat16),
            pltpu.VMEM((4,) + momentum_down.shape, f32),
            pltpu.VMEM((2, lowrank, tokens), f32),
            pltpu.VMEM((n, 2, lowrank, tokens), f32),
            pltpu.VMEM((2, tokens, w), f32),
            pltpu.VMEM((2, tokens, w), f32),
            pltpu.VMEM((2, lowrank, tokens), f32),
            pltpu.VMEM((2, lowrank, tokens), f32),
            pltpu.VMEM((n, 2, lowrank, w), f32),
            pltpu.VMEM((n, 2, lowrank, w), f32),
            pltpu.VMEM((n, 2, lowrank, w), f32),
            pltpu.VMEM((tenants, 2, lowrank, w), f32),
            pltpu.VMEM((line, tokens, w), f32),
            pltpu.VMEM((line, tokens, w), f32),
            pltpu.VMEM((line, tokens, w), f32),
            pltpu.VMEM((line, tokens, w), f32),
            pltpu.VMEM((line, tokens, w), f32),
            pltpu.VMEM((tokens, w), f32),
            pltpu.VMEM((2, 2, lowrank, w), f32),
            pltpu.VMEM((8, 128), f32),
            pltpu.VMEM((2, 8, 128), f32),
            dma((6,)),
            dma((3,)),
            dma((n,)),
            dma((1,)),
            dma((1,)),
            dma((n,)),
            dma((3,)),
            dma((4,)),
            dma((1,)),
            dma((n,)),
            dma((1,)),
            dma((n,)),
            dma((1,)),
            dma((n,)),
            dma((1,)),
            dma((line * CHUNKS,)),
            dma((1,)),
            dma(((line + 1) * CHUNKS,)),
            dma((1,)),
            dma((2,)),
            dma((2,)),
            dma((2,)),
        ],
        compiler_params=pltpu.CompilerParams(
            collective_id=0, has_side_effects=True, vmem_limit_bytes=48 * 1024 * 1024
        ),
    )(
        *(
            pltpu.with_memory_space_constraint(x, pltpu.HBM)
            for x in (
                owner_device,
                token_tenant.reshape(1, tokens),
                features,
                cotangent,
                adapter_down,
                adapter_up,
                frozen_weight,
                momentum_down,
                momentum_up,
                variance_down,
                variance_up,
            )
        )
    )
    return pl.pallas_call(
        hand_out,
        out_shape=tuple(shape(r.shape, r.dtype) for r in results),
        in_specs=[anywhere] * len(results),
        out_specs=[hbm] * len(results),
        scratch_shapes=[dma((len(results),))],
        compiler_params=pltpu.CompilerParams(vmem_limit_bytes=1024 * 1024),
    )(*results)


def solution(mesh):
    in_specs = (
        P(("group", "dp"), "tensor"),
        P(("group", "dp"), "tensor"),
        P(("group", "dp")),
        P("group"),
        P("tensor", None),
        P("group", None, "tensor"),
        P("group", None, "tensor"),
        P(("group", "tensor", "dp"), None, None),
        P(("group", "tensor", "dp"), None, None),
        P(("group", "tensor", "dp"), None, None),
        P(("group", "tensor", "dp"), None, None),
    )
    out_specs = (
        P(("group", "dp"), "tensor"),
        P("group", None, "tensor"),
        P("group", None, "tensor"),
        P(("group", "tensor", "dp"), None, None),
        P(("group", "tensor", "dp"), None, None),
        P(("group", "tensor", "dp"), None, None),
        P(("group", "tensor", "dp"), None, None),
    )
    return jax.shard_map(
        functools.partial(on_device, mesh.shape["tensor"]),
        mesh=mesh,
        in_specs=in_specs,
        out_specs=out_specs,
        check_vma=False,
    )
```

```python
import functools

import jax
import jax.numpy as jnp
from jax import lax
from jax.experimental import pallas as pl
from jax.experimental.pallas import tpu as pltpu
from jax.sharding import PartitionSpec as P

MESH = pl.DeviceIdType.MESH

adapter_scale = 2.0
clip_norm = 12000.0
learn_rate = 0.004
beta_one = 0.9
beta_two = 0.999
adam_eps = 1e-08
correct_one = 1.0 - beta_one**20
correct_two = 1.0 - beta_two**20

CHUNKS = 4
EARLY = 1
LEND_AT = 1
INNER = ((1, 0), (1, 1), (2, 0), (2, 1), (1, 2), (2, 2), (1, 3), (2, 3))


def adam_step(gradient, factor, moment, square):
    clipped = gradient * factor
    moment_next = beta_one * moment + (1.0 - beta_one) * clipped
    square_next = beta_two * square + (1.0 - beta_two) * clipped * clipped
    change = (
        learn_rate * (moment_next / correct_one) / (jnp.sqrt(square_next / correct_two) + adam_eps)
    )
    return (moment_next, square_next, change)


def block_order(line, zi):
    low = zi < line // 2
    near = jnp.where(low, zi, line - 1 - zi)
    order = []
    for k in range(line - 1):
        far_first = line - 1 - (k // 2 if k % 2 == 0 else k // 2)
        paired = far_first if k % 2 == 0 else k // 2
        alone = line - 1 - (k - near)
        place = jnp.where(k < 2 * near, paired, alone)
        order.append(jnp.where(low, place, line - 1 - place))
    order.append(zi)
    return order


def kernel(
    n,
    owner_hbm,
    tenant_hbm,
    feat_hbm,
    cot_hbm,
    down_hbm,
    up_hbm,
    weight_ref,
    mom_down_ref,
    mom_up_ref,
    var_down_ref,
    var_up_ref,
    proj_hbm,
    new_down_hbm,
    new_up_hbm,
    mean_down_ref,
    mean_up_ref,
    power_down_ref,
    power_up_ref,
    owner_ref,
    tenant_ref,
    mate_tenant,
    rows_ref,
    down_ref,
    up_ref,
    proj_ref,
    new_down_ref,
    new_up_ref,
    wbuf,
    state,
    rpart,
    rbuf,
    raw_out,
    raw_in,
    low_out,
    low_in,
    summed,
    owned,
    change,
    changes,
    ysend,
    yrecv,
    part,
    going_up,
    going_down,
    adapted,
    lent,
    scale_out,
    scale_in,
    isem,
    osem,
    wsem,
    msem,
    rank_s,
    rank_r,
    g_s,
    g_r,
    a_s,
    a_r,
    c_s,
    c_r,
    f_s,
    f_r,
    y_s,
    y_r,
    z_s,
    z_r,
    l_s,
    l_r,
    h_s,
    s_r,
):
    tenants, lowrank, w = down_ref.shape
    tokens = tenant_ref.shape[1]
    feat_ref, cot_ref = (rows_ref.at[i, pl.ds(0, tokens)] for i in range(2))
    line = n // 2
    t = lax.axis_index("tensor")
    d = lax.axis_index("dp")
    zi, yi = t // 2, lax.rem(t, 2)
    mate = {"dp": 1 - d}
    pair = {"tensor": zi * 2 + 1 - yi}
    order = block_order(line, zi)
    height = tokens // CHUNKS
    low_side = zi < line // 2
    lent_to = jnp.where(low_side, t + 2, t - 2)
    lent_way = jnp.where(low_side, 0, 1)
    from_below = jnp.logical_and(zi > 0, zi - 1 < line // 2)
    from_above = jnp.logical_and(zi < line - 1, zi + 1 >= line // 2)
    paired = n & (n - 1) == 0

    def peer(o):
        return t ^ (n - o) if paired else lax.rem(t + o, n)

    def giver(o):
        return t ^ (n - o) if paired else lax.rem(t + n - o, n)

    def columns(block):
        return pl.ds(pl.multiple_of(block * w, w), w)

    def sent(ref, sem):
        pltpu.make_async_copy(ref, ref, sem).wait()

    barrier = pltpu.get_barrier_semaphore()

    in_copies = [
        pltpu.make_async_copy(src, dst, isem.at[i])
        for i, (src, dst) in enumerate(
            (
                (tenant_hbm, tenant_ref),
                (cot_hbm, cot_ref),
                (up_hbm, up_ref),
                (feat_hbm, feat_ref),
                (down_hbm, down_ref),
                (owner_hbm, owner_ref),
            )
        )
    ]
    for copy in in_copies:
        copy.start()

    @pl.loop(1, n)
    def _(o):
        pl.semaphore_signal(barrier, inc=1, device_id={"tensor": peer(o)}, device_id_type=MESH)

    pl.semaphore_signal(barrier, inc=1, device_id=mate, device_id_type=MESH)

    def weight_copy(i, block):
        return pltpu.make_async_copy(
            weight_ref.at[:, columns(block)], wbuf.at[i], wsem.at[i]
        )

    blocks = [z * 2 + 1 - yi for z in order] + [z * 2 + yi for z in order]
    in_copies[0].wait()
    tenant = tenant_ref[...]
    contract = (((1,), (1,)), ((), ()))
    tenant_row = lax.broadcasted_iota(jnp.int32, (tenants, lowrank, tokens), 0)
    tenant_hit = tenant_row == tenant[None]

    def rank_part(adapter, rows):
        scores = lax.dot_general(
            adapter[...].reshape(tenants * lowrank, w),
            rows[...],
            contract,
            preferred_element_type=jnp.float32,
        ).reshape(tenants, lowrank, tokens)
        return jnp.sum(jnp.where(tenant_hit, scores, 0.0), axis=0)

    for copy in in_copies[1:3]:
        copy.wait()
    rpart[0] = rank_part(up_ref, cot_ref)
    for copy in in_copies[3:]:
        copy.wait()
    for i, block in enumerate(blocks):
        weight_copy(i, block).start()
    state_copies = [
        pltpu.make_async_copy(ref, state.at[i], msem.at[0])
        for i, ref in enumerate((mom_down_ref, mom_up_ref, var_down_ref, var_up_ref))
    ]
    for copy in state_copies:
        copy.start()
    pl.semaphore_wait(barrier, n)

    def rank_copy(o, source, side):
        return pltpu.make_async_remote_copy(
            src_ref=rpart.at[side],
            dst_ref=rbuf.at[side, source],
            send_sem=rank_s.at[0],
            recv_sem=rank_r.at[side],
            device_id={"tensor": peer(o)},
            device_id_type=MESH,
        )

    @pl.loop(1, n)
    def _(o):
        rank_copy(o, t, 0).start()

    rpart[1] = rank_part(down_ref, feat_ref)

    @pl.loop(1, n)
    def _(o):
        rank_copy(o, t, 1).start()

    def mate_copy(source, target, out, arrived):
        return pltpu.make_async_remote_copy(
            src_ref=source,
            dst_ref=target,
            send_sem=g_s.at[out],
            recv_sem=g_r.at[arrived],
            device_id=mate,
            device_id_type=MESH,
        )

    tenant_copy = mate_copy(tenant_ref, mate_tenant, 0, 0)
    raw_copies = [mate_copy(raw_out.at[i], raw_in.at[i], 1, 1 + i) for i in range(2)]
    low_copies = [mate_copy(low_out.at[i], low_in.at[i], 2 + i, 3 + i) for i in range(2)]
    tenant_copy.start()
    for i, rows in enumerate((feat_ref, cot_ref)):
        raw_out[i] = rows[...].astype(jnp.float32)
        raw_copies[i].start()

    def lent_copy(i):
        return pltpu.make_async_remote_copy(
            src_ref=(mom_down_ref, var_down_ref)[i].at[0, :, columns(lent_to)],
            dst_ref=lent.at[lent_way, i],
            send_sem=l_s.at[0],
            recv_sem=l_r.at[lent_way],
            device_id={"tensor": lent_to},
            device_id_type=MESH,
        )

    def rows_of(c):
        return pl.ds(c * height, height)

    def pair_copy(z, c):
        return pltpu.make_async_remote_copy(
            src_ref=ysend.at[z, rows_of(c)],
            dst_ref=yrecv.at[z, rows_of(c)],
            send_sem=y_s.at[0],
            recv_sem=y_r.at[z * CHUNKS + c],
            device_id=pair,
            device_id_type=MESH,
        )

    def pair_start(z):
        for c in range(CHUNKS):
            pair_copy(z, c).start()

    def frozen(i):
        sent(wbuf.at[i], wsem.at[i])
        return jnp.dot(feat_ref[...], wbuf[i], preferred_element_type=jnp.float32)

    for i, z in enumerate(order):
        ysend[z] = frozen(i)
        if i == 0:
            pair_start(z)
        if i == LEND_AT:
            for k in range(2):
                lent_copy(k).start()

    tenant_copy.wait_recv()
    tenants_here = (tenant, mate_tenant[...])
    slots = lax.fori_loop(
        0,
        tenants,
        lambda k, found: tuple(
            jnp.where(here == k, owner_ref[k], s) for here, s in zip(tenants_here, found)
        ),
        tuple(jnp.zeros_like(here) for here in tenants_here),
    )
    for i in range(2):
        raw_copies[i].wait_recv()
        rows_ref[i, tokens:] = raw_in[i].astype(jnp.bfloat16)

    half_row = lax.broadcasted_iota(jnp.int32, (n, lowrank, tokens), 0) * 2 + d

    def spread(values, slot):
        picked = jnp.where(half_row == slot[None], values[None], 0.0)
        return picked.reshape(n * lowrank, tokens).astype(jnp.bfloat16)

    def grad_copy(o, source, side):
        return pltpu.make_async_remote_copy(
            src_ref=summed.at[peer(o), side],
            dst_ref=owned.at[source, side],
            send_sem=a_s.at[0],
            recv_sem=a_r.at[0],
            device_id={"tensor": peer(o)},
            device_id_type=MESH,
        )

    lows = []
    for i in range(2):
        sent(rbuf.at[i, pl.ds(0, n - 1)], rank_r.at[i])
        rbuf[i, t] = rpart[i]
        total = rbuf[i, 0]
        for source in range(1, n):
            total = total + rbuf[i, source]
        low = (adapter_scale * total).astype(jnp.bfloat16).astype(jnp.float32)
        low_out[i] = low
        low_copies[i].start()
        own_part = spread(low, slots[0])
        lows.append(low)
        low_copies[i].wait_recv()
        summed[:, i] = jnp.dot(
            jnp.concatenate([own_part, spread(low_in[i], slots[1])], axis=1),
            rows_ref[i],
            preferred_element_type=jnp.float32,
        ).reshape(n, lowrank, w)

        @pl.loop(1, n)
        def _(o):
            grad_copy(o, t, i).start()

    down_low = lows[1]

    pair_start(order[1])

    owned[t] = summed[t]

    down_spread = jnp.where(tenant_hit, down_low[None], 0.0).reshape(tenants * lowrank, tokens)
    adapted[...] = jnp.dot(
        jnp.transpose(down_spread).astype(jnp.bfloat16),
        up_ref[...].reshape(tenants * lowrank, w),
        preferred_element_type=jnp.float32,
    )
    for i, z in enumerate(order):
        part[z] = frozen(line + i)

    def up_copy(z, c):
        return pltpu.make_async_remote_copy(
            src_ref=part.at[z, rows_of(c)],
            dst_ref=going_up.at[z, rows_of(c)],
            send_sem=z_s.at[0],
            recv_sem=z_r.at[z * CHUNKS + c],
            device_id={"tensor": lax.rem(t + 2, n)},
            device_id_type=MESH,
        )

    def down_copy(z, c, last=False):
        slot_at = line if last else z
        return pltpu.make_async_remote_copy(
            src_ref=part.at[z, rows_of(c)],
            dst_ref=going_down.at[z, rows_of(c)],
            send_sem=z_s.at[0],
            recv_sem=z_r.at[slot_at * CHUNKS + c],
            device_id={"tensor": lax.rem(t + n - 2, n)},
            device_id_type=MESH,
        )

    def send_down(z, c):
        @pl.when(z == zi - 1)
        def _():
            down_copy(z, c, True).start()

        @pl.when(z < zi - 1)
        def _():
            down_copy(z, c).start()

    def pair_add(z, c):
        at = rows_of(c)
        pair_copy(z, c).wait_recv()
        part[z, at] = part[z, at] + yrecv[z, at]

    def ends(z, c):
        @pl.when(jnp.logical_and(zi == 0, z > 0))
        def _():
            up_copy(z, c).start()

        @pl.when(jnp.logical_and(zi == line - 1, z < line - 1))
        def _():
            send_down(z, c)

    def middles(z, c):
        at = rows_of(c)

        @pl.when(jnp.logical_and(zi > 0, zi < z))
        def _():
            up_copy(z, c).wait_recv()
            part[z, at] = part[z, at] + going_up[z, at]
            up_copy(z, c).start()

        @pl.when(jnp.logical_and(zi > z, zi < line - 1))
        def _():
            down_copy(z, c).wait_recv()
            part[z, at] = part[z, at] + going_down[z, at]
            send_down(z, c)

    for c in range(CHUNKS):
        pair_add(order[0], c)
        ends(order[0], c)
    for c in range(EARLY):
        middles(order[0], c)

    sent(state, msem.at[0])

    sent(owned.at[pl.ds(0, n - 1)], a_r.at[0])

    def squares_of(k, acc):
        g = owned[k]
        return acc + jnp.sum(g * g, axis=0)

    squares = lax.fori_loop(0, n, squares_of, jnp.zeros((lowrank, w), jnp.float32))
    squares = jnp.sum(squares, axis=(0, 1), keepdims=True)
    factor = clip_norm / jnp.maximum(jnp.sqrt(squares), clip_norm)

    def change_copy(o, source):
        return pltpu.make_async_remote_copy(
            src_ref=change.at[peer(o)],
            dst_ref=changes.at[source * 2 + d],
            send_sem=c_s.at[0],
            recv_sem=c_r.at[source],
            device_id={"tensor": peer(o)},
            device_id_type=MESH,
        )

    def half_copy(source):
        return pltpu.make_async_remote_copy(
            src_ref=change.at[lent_to, 1],
            dst_ref=changes.at[source * 2 + d, 1],
            send_sem=h_s.at[0],
            recv_sem=c_r.at[source],
            device_id={"tensor": lent_to},
            device_id_type=MESH,
        )

    scale_copy = pltpu.make_async_remote_copy(
        src_ref=scale_out,
        dst_ref=scale_in.at[lent_way],
        send_sem=h_s.at[1],
        recv_sem=s_r.at[lent_way],
        device_id={"tensor": lent_to},
        device_id_type=MESH,
    )
    scale_out[...] = jnp.broadcast_to(factor, scale_out.shape)
    scale_copy.start()

    def change_start(o):
        @pl.when(peer(o) != lent_to)
        def _():
            change_copy(o, t).start()

        @pl.when(peer(o) == lent_to)
        def _():
            half_copy(t).start()

    def step_piece(k):
        at = columns(k)
        for i in range(2):
            mean, power, moved = adam_step(
                owned[k, i], factor, state[i, 0, :, at], state[2 + i, 0, :, at]
            )
            state[i, 0, :, at] = mean
            state[2 + i, 0, :, at] = power
            change[k, i] = moved

    @pl.loop(1, n)
    def _(o):
        step_piece(peer(o))

        @pl.when(o > 1)
        def _():
            change_start(o - 1)

    step_piece(t)
    change_start(n - 1)
    changes[t * 2 + d] = change[t]

    for z in order[2:]:
        pair_start(z)

    def forward_copy(source, side):
        at = source * 2 + side
        return pltpu.make_async_remote_copy(
            src_ref=changes.at[at],
            dst_ref=changes.at[at],
            send_sem=f_s.at[0],
            recv_sem=f_r.at[0],
            device_id=mate,
            device_id_type=MESH,
        )

    forward_copy(t, d).start()
    state_outs = [
        pltpu.make_async_copy(state.at[i], ref, msem.at[0])
        for i, ref in enumerate((mean_down_ref, mean_up_ref, power_down_ref, power_up_ref))
    ]
    for copy in state_outs:
        copy.start()

    inner = jnp.logical_and(zi > 0, zi < line - 1)

    @pl.when(inner)
    def _():
        for c in range(EARLY, CHUNKS):
            middles(order[0], c)
        for k, c in INNER:
            pair_add(order[k], c)
            middles(order[k], c)

    @pl.when(jnp.logical_not(inner))
    def _():
        for k in (1, 2):
            for c in range(CHUNKS):
                pair_add(order[k], c)
                ends(order[k], c)

    for z in order[3:-1]:
        for c in range(CHUNKS):
            pair_add(z, c)
            ends(z, c)
            middles(z, c)

    @pl.loop(1, n)
    def _(o):
        source = giver(o)
        below = jnp.logical_and(from_below, source == t - 2)
        above = jnp.logical_and(from_above, source == t + 2)
        borrowed = jnp.logical_or(below, above)

        @pl.when(jnp.logical_not(borrowed))
        def _():
            change_copy(o, source).wait_recv()

        @pl.when(borrowed)
        def _():
            way = jnp.where(below, 0, 1)
            half_copy(source).wait_recv()
            sent(scale_in.at[way], s_r.at[way])
            sent(lent.at[way], l_r.at[way])
            scale = scale_in[way]
            changes[source * 2 + d, 0] = adam_step(
                summed[source, 0], scale[:1, :1], lent[way, 0], lent[way, 1]
            )[2]

        forward_copy(source, d).start()

    sent(changes.at[pl.ds(0, n)], f_r.at[0])

    @pl.loop(0, tenants)
    def _(k):
        back = changes[owner_ref[k]]
        new_down_ref[k] = (down_ref[k].astype(jnp.float32) - back[0]).astype(jnp.bfloat16)
        new_up_ref[k] = (up_ref[k].astype(jnp.float32) - back[1]).astype(jnp.bfloat16)

    adapter_outs = [
        pltpu.make_async_copy(new_down_ref, new_down_hbm, osem.at[0]),
        pltpu.make_async_copy(new_up_ref, new_up_hbm, osem.at[1]),
    ]
    for copy in adapter_outs:
        copy.start()

    def proj_out(c):
        at = rows_of(c)
        return pltpu.make_async_copy(proj_ref.at[at], proj_hbm.at[at], osem.at[2])

    for c in range(CHUNKS):
        at = rows_of(c)
        pair_add(zi, c)

        @pl.when(zi > 0)
        def _():
            up_copy(zi, c).wait_recv()
            part[zi, at] = part[zi, at] + going_up[zi, at]

        @pl.when(zi < line - 1)
        def _():
            down_copy(zi, c, True).wait_recv()
            part[zi, at] = part[zi, at] + going_down[zi, at]

        proj_ref[at] = (part[zi, at] + adapted[at]).astype(proj_ref.dtype)
        proj_out(c).start()

    sent(state, msem.at[0])
    for copy in adapter_outs:
        copy.wait()

    sent(rbuf.at[:, pl.ds(0, n - 1)], rank_s.at[0])
    tenant_copy.wait_send()
    sent(raw_out, g_s.at[1])
    for copy in low_copies:
        copy.wait_send()
    sent(change.at[pl.ds(0, n - 1)], a_s.at[0])
    sent(change.at[pl.ds(0, n - 2)], c_s.at[0])
    sent(change.at[0, 0], h_s.at[0])
    sent(scale_out, h_s.at[1])
    sent(lent.at[0], l_s.at[0])
    sent(changes.at[pl.ds(0, n)], f_s.at[0])
    sent(ysend, y_s.at[0])
    sent(part.at[pl.ds(0, line - 1)], z_s.at[0])
    sent(proj_ref, osem.at[2])


def hand_out(*refs):
    count = len(refs) // 2
    sems = refs[-1]
    outs = [pltpu.make_async_copy(refs[i], refs[count + i], sems.at[i]) for i in range(count)]
    for copy in outs:
        copy.start()
    for copy in outs:
        copy.wait()


def on_device(n, *args):
    (
        features,
        cotangent,
        token_tenant,
        owner_device,
        frozen_weight,
        adapter_down,
        adapter_up,
        momentum_down,
        momentum_up,
        variance_down,
        variance_up,
    ) = args
    tokens, depth = features.shape
    tenants, lowrank, w = adapter_down.shape
    line = n // 2
    f32 = jnp.float32
    bf16 = jnp.bfloat16
    hbm = pl.BlockSpec(memory_space=pltpu.HBM)
    anywhere = pl.BlockSpec(memory_space=pl.ANY)
    dma = pltpu.SemaphoreType.DMA
    shape = jax.ShapeDtypeStruct
    results = pl.pallas_call(
        functools.partial(kernel, n),
        out_shape=(
            shape((tokens, w), jnp.bfloat16),
            shape(adapter_down.shape, jnp.bfloat16),
            shape(adapter_up.shape, jnp.bfloat16),
            shape(momentum_down.shape, f32),
            shape(momentum_up.shape, f32),
            shape(variance_down.shape, f32),
            shape(variance_up.shape, f32),
        ),
        in_specs=[hbm] * 11,
        out_specs=[anywhere] * 7,
        scratch_shapes=[
            pltpu.SMEM((tenants,), jnp.int32),
            pltpu.VMEM((1, tokens), jnp.int32),
            pltpu.VMEM((1, tokens), jnp.int32),
            pltpu.VMEM((2, 2 * tokens, w), bf16),
            pltpu.VMEM(adapter_down.shape, bf16),
            pltpu.VMEM(adapter_up.shape, bf16),
            pltpu.VMEM((tokens, w), bf16),
            pltpu.VMEM(adapter_down.shape, bf16),
            pltpu.VMEM(adapter_up.shape, bf16),
            pltpu.VMEM((n, depth, w), jnp.bfloat16),
            pltpu.VMEM((4,) + momentum_down.shape, f32),
            pltpu.VMEM((2, lowrank, tokens), f32),
            pltpu.VMEM((2, n, lowrank, tokens), f32),
            pltpu.VMEM((2, tokens, w), f32),
            pltpu.VMEM((2, tokens, w), f32),
            pltpu.VMEM((2, lowrank, tokens), f32),
            pltpu.VMEM((2, lowrank, tokens), f32),
            pltpu.VMEM((n, 2, lowrank, w), f32),
            pltpu.VMEM((n, 2, lowrank, w), f32),
            pltpu.VMEM((n, 2, lowrank, w), f32),
            pltpu.VMEM((tenants, 2, lowrank, w), f32),
            pltpu.VMEM((line, tokens, w), f32),
            pltpu.VMEM((line, tokens, w), f32),
            pltpu.VMEM((line, tokens, w), f32),
            pltpu.VMEM((line, tokens, w), f32),
            pltpu.VMEM((line, tokens, w), f32),
            pltpu.VMEM((tokens, w), f32),
            pltpu.VMEM((2, 2, lowrank, w), f32),
            pltpu.VMEM((8, 128), f32),
            pltpu.VMEM((2, 8, 128), f32),
            dma((6,)),
            dma((3,)),
            dma((n,)),
            dma((1,)),
            dma((1,)),
            dma((2,)),
            dma((4,)),
            dma((5,)),
            dma((1,)),
            dma((1,)),
            dma((1,)),
            dma((n,)),
            dma((1,)),
            dma((1,)),
            dma((1,)),
            dma((line * CHUNKS,)),
            dma((1,)),
            dma(((line + 1) * CHUNKS,)),
            dma((1,)),
            dma((2,)),
            dma((2,)),
            dma((2,)),
        ],
        compiler_params=pltpu.CompilerParams(
            collective_id=0, has_side_effects=True, vmem_limit_bytes=48 * 1024 * 1024
        ),
    )(
        *(
            pltpu.with_memory_space_constraint(x, pltpu.HBM)
            for x in (
                owner_device,
                token_tenant.reshape(1, tokens),
                features,
                cotangent,
                adapter_down,
                adapter_up,
                frozen_weight,
                momentum_down,
                momentum_up,
                variance_down,
                variance_up,
            )
        )
    )
    return pl.pallas_call(
        hand_out,
        out_shape=tuple(shape(r.shape, r.dtype) for r in results),
        in_specs=[anywhere] * len(results),
        out_specs=[hbm] * len(results),
        scratch_shapes=[dma((len(results),))],
        compiler_params=pltpu.CompilerParams(vmem_limit_bytes=1024 * 1024),
    )(*results)


def solution(mesh):
    in_specs = (
        P(("group", "dp"), "tensor"),
        P(("group", "dp"), "tensor"),
        P(("group", "dp")),
        P("group"),
        P("tensor", None),
        P("group", None, "tensor"),
        P("group", None, "tensor"),
        P(("group", "tensor", "dp"), None, None),
        P(("group", "tensor", "dp"), None, None),
        P(("group", "tensor", "dp"), None, None),
        P(("group", "tensor", "dp"), None, None),
    )
    out_specs = (
        P(("group", "dp"), "tensor"),
        P("group", None, "tensor"),
        P("group", None, "tensor"),
        P(("group", "tensor", "dp"), None, None),
        P(("group", "tensor", "dp"), None, None),
        P(("group", "tensor", "dp"), None, None),
        P(("group", "tensor", "dp"), None, None),
    )
    return jax.shard_map(
        functools.partial(on_device, mesh.shape["tensor"]),
        mesh=mesh,
        in_specs=in_specs,
        out_specs=out_specs,
        check_vma=False,
    )
```

```python
import functools

import jax
import jax.numpy as jnp
from jax import lax
from jax.experimental import pallas as pl
from jax.experimental.pallas import tpu as pltpu
from jax.sharding import PartitionSpec as P

MESH = pl.DeviceIdType.MESH

adapter_scale = 2.0
clip_norm = 12000.0
learn_rate = 0.004
beta_one = 0.9
beta_two = 0.999
adam_eps = 1e-08
correct_one = 1.0 - beta_one**20
correct_two = 1.0 - beta_two**20

CHUNKS = 4
EARLY = 1
LEND_AT = 1
INNER = ((1, 0), (1, 1), (2, 0), (2, 1), (1, 2), (2, 2), (1, 3), (2, 3))


def adam_step(gradient, factor, moment, square):
    clipped = gradient * factor
    moment_next = beta_one * moment + (1.0 - beta_one) * clipped
    square_next = beta_two * square + (1.0 - beta_two) * clipped * clipped
    change = (
        learn_rate * (moment_next / correct_one) / (jnp.sqrt(square_next / correct_two) + adam_eps)
    )
    return (moment_next, square_next, change)


def block_order(line, zi):
    low = zi < line // 2
    near = jnp.where(low, zi, line - 1 - zi)
    order = []
    for k in range(line - 1):
        far_first = line - 1 - (k // 2 if k % 2 == 0 else k // 2)
        paired = far_first if k % 2 == 0 else k // 2
        alone = line - 1 - (k - near)
        place = jnp.where(k < 2 * near, paired, alone)
        order.append(jnp.where(low, place, line - 1 - place))
    order.append(zi)
    return order


def kernel(
    n,
    owner_hbm,
    tenant_hbm,
    feat_hbm,
    cot_hbm,
    down_hbm,
    up_hbm,
    weight_ref,
    mom_down_ref,
    mom_up_ref,
    var_down_ref,
    var_up_ref,
    proj_hbm,
    new_down_hbm,
    new_up_hbm,
    mean_down_ref,
    mean_up_ref,
    power_down_ref,
    power_up_ref,
    owner_ref,
    tenant_ref,
    mate_tenant,
    rows_ref,
    down_ref,
    up_ref,
    proj_ref,
    new_down_ref,
    new_up_ref,
    wbuf,
    state,
    rpart,
    rbuf,
    raw_out,
    raw_in,
    low_out,
    low_in,
    summed,
    owned,
    change,
    changes,
    ysend,
    yrecv,
    part,
    going_up,
    going_down,
    adapted,
    lent,
    scale_out,
    scale_in,
    isem,
    osem,
    wsem,
    msem,
    rank_s,
    rank_r,
    g_s,
    g_r,
    a_s,
    a_r,
    c_s,
    c_r,
    f_s,
    f_r,
    y_s,
    y_r,
    z_s,
    z_r,
    l_s,
    l_r,
    h_s,
    s_r,
):
    tenants, lowrank, w = down_ref.shape
    tokens = tenant_ref.shape[1]
    feat_ref, cot_ref = (rows_ref.at[i, pl.ds(0, tokens)] for i in range(2))
    line = n // 2
    t = lax.axis_index("tensor")
    d = lax.axis_index("dp")
    zi, yi = t // 2, lax.rem(t, 2)
    mate = {"dp": 1 - d}
    pair = {"tensor": zi * 2 + 1 - yi}
    order = block_order(line, zi)
    height = tokens // CHUNKS
    low_side = zi < line // 2
    lent_to = jnp.where(low_side, t + 2, t - 2)
    lent_way = jnp.where(low_side, 0, 1)
    from_below = jnp.logical_and(zi > 0, zi - 1 < line // 2)
    from_above = jnp.logical_and(zi < line - 1, zi + 1 >= line // 2)
    paired = n & (n - 1) == 0

    def peer(o):
        return t ^ (n - o) if paired else lax.rem(t + o, n)

    def giver(o):
        return t ^ (n - o) if paired else lax.rem(t + n - o, n)

    def columns(block):
        return pl.ds(pl.multiple_of(block * w, w), w)

    def sent(ref, sem):
        pltpu.make_async_copy(ref, ref, sem).wait()

    barrier = pltpu.get_barrier_semaphore()

    in_copies = [
        pltpu.make_async_copy(src, dst, isem.at[i])
        for i, (src, dst) in enumerate(
            (
                (tenant_hbm, tenant_ref),
                (cot_hbm, cot_ref),
                (up_hbm, up_ref),
                (feat_hbm, feat_ref),
                (down_hbm, down_ref),
                (owner_hbm, owner_ref),
            )
        )
    ]
    for copy in in_copies:
        copy.start()

    @pl.loop(1, n)
    def _(o):
        pl.semaphore_signal(barrier, inc=1, device_id={"tensor": peer(o)}, device_id_type=MESH)

    pl.semaphore_signal(barrier, inc=1, device_id=mate, device_id_type=MESH)

    def weight_copy(i, block):
        return pltpu.make_async_copy(
            weight_ref.at[:, columns(block)], wbuf.at[i], wsem.at[i]
        )

    blocks = [z * 2 + 1 - yi for z in order] + [z * 2 + yi for z in order]
    in_copies[0].wait()
    tenant = tenant_ref[...]
    contract = (((1,), (1,)), ((), ()))
    tenant_row = lax.broadcasted_iota(jnp.int32, (tenants, lowrank, tokens), 0)
    tenant_hit = tenant_row == tenant[None]

    def rank_part(adapter, rows):
        scores = lax.dot_general(
            adapter[...].reshape(tenants * lowrank, w),
            rows[...],
            contract,
            preferred_element_type=jnp.float32,
        ).reshape(tenants, lowrank, tokens)
        return jnp.sum(jnp.where(tenant_hit, scores, 0.0), axis=0)

    for copy in in_copies[1:3]:
        copy.wait()
    rpart[0] = rank_part(up_ref, cot_ref)
    for copy in in_copies[3:]:
        copy.wait()
    for i, block in enumerate(blocks):
        weight_copy(i, block).start()
    state_copies = [
        pltpu.make_async_copy(ref, state.at[i], msem.at[0])
        for i, ref in enumerate((mom_down_ref, mom_up_ref, var_down_ref, var_up_ref))
    ]
    for copy in state_copies:
        copy.start()
    pl.semaphore_wait(barrier, n)

    def rank_copy(o, source, side):
        return pltpu.make_async_remote_copy(
            src_ref=rpart.at[side],
            dst_ref=rbuf.at[side, source],
            send_sem=rank_s.at[0],
            recv_sem=rank_r.at[side],
            device_id={"tensor": peer(o)},
            device_id_type=MESH,
        )

    @pl.loop(1, n)
    def _(o):
        rank_copy(o, t, 0).start()

    rpart[1] = rank_part(down_ref, feat_ref)

    @pl.loop(1, n)
    def _(o):
        rank_copy(o, t, 1).start()

    def mate_copy(source, target, out, arrived):
        return pltpu.make_async_remote_copy(
            src_ref=source,
            dst_ref=target,
            send_sem=g_s.at[out],
            recv_sem=g_r.at[arrived],
            device_id=mate,
            device_id_type=MESH,
        )

    tenant_copy = mate_copy(tenant_ref, mate_tenant, 0, 0)
    raw_copies = [mate_copy(raw_out.at[i], raw_in.at[i], 1, 1 + i) for i in range(2)]
    low_copies = [mate_copy(low_out.at[i], low_in.at[i], 2 + i, 3 + i) for i in range(2)]
    tenant_copy.start()
    for i, rows in enumerate((feat_ref, cot_ref)):
        raw_out[i] = rows[...].astype(jnp.float32)
        raw_copies[i].start()

    def lent_copy(i):
        return pltpu.make_async_remote_copy(
            src_ref=(mom_down_ref, var_down_ref)[i].at[0, :, columns(lent_to)],
            dst_ref=lent.at[lent_way, i],
            send_sem=l_s.at[0],
            recv_sem=l_r.at[lent_way],
            device_id={"tensor": lent_to},
            device_id_type=MESH,
        )

    def rows_of(c):
        return pl.ds(c * height, height)

    def pair_copy(z, c):
        return pltpu.make_async_remote_copy(
            src_ref=ysend.at[z, rows_of(c)],
            dst_ref=yrecv.at[z, rows_of(c)],
            send_sem=y_s.at[0],
            recv_sem=y_r.at[z * CHUNKS + c],
            device_id=pair,
            device_id_type=MESH,
        )

    def pair_start(z, first=0, last=CHUNKS):
        for c in range(first, last):
            pair_copy(z, c).start()

    def frozen(i):
        sent(wbuf.at[i], wsem.at[i])
        return jnp.dot(feat_ref[...], wbuf[i], preferred_element_type=jnp.float32)

    for i, z in enumerate(order):
        ysend[z] = frozen(i)
        if i == 0:
            pair_start(z, 0, 2)
        if i == LEND_AT:
            for k in range(2):
                lent_copy(k).start()

    tenant_copy.wait_recv()
    tenants_here = (tenant, mate_tenant[...])
    slots = lax.fori_loop(
        0,
        tenants,
        lambda k, found: tuple(
            jnp.where(here == k, owner_ref[k], s) for here, s in zip(tenants_here, found)
        ),
        tuple(jnp.zeros_like(here) for here in tenants_here),
    )
    for i in range(2):
        raw_copies[i].wait_recv()
        rows_ref[i, tokens:] = raw_in[i].astype(jnp.bfloat16)

    half_row = lax.broadcasted_iota(jnp.int32, (n, lowrank, tokens), 0) * 2 + d

    def spread(values, slot):
        picked = jnp.where(half_row == slot[None], values[None], 0.0)
        return picked.reshape(n * lowrank, tokens).astype(jnp.bfloat16)

    def grad_copy(o, source, side):
        return pltpu.make_async_remote_copy(
            src_ref=summed.at[peer(o), side],
            dst_ref=owned.at[source, side],
            send_sem=a_s.at[0],
            recv_sem=a_r.at[0],
            device_id={"tensor": peer(o)},
            device_id_type=MESH,
        )

    lows = []
    for i in range(2):
        sent(rbuf.at[i, pl.ds(0, n - 1)], rank_r.at[i])
        rbuf[i, t] = rpart[i]
        total = rbuf[i, 0]
        for source in range(1, n):
            total = total + rbuf[i, source]
        low = (adapter_scale * total).astype(jnp.bfloat16).astype(jnp.float32)
        low_out[i] = low
        low_copies[i].start()
        own_part = spread(low, slots[0])
        lows.append(low)
        low_copies[i].wait_recv()
        summed[:, i] = jnp.dot(
            jnp.concatenate([own_part, spread(low_in[i], slots[1])], axis=1),
            rows_ref[i],
            preferred_element_type=jnp.float32,
        ).reshape(n, lowrank, w)

        @pl.loop(1, n)
        def _(o):
            grad_copy(o, t, i).start()

    down_low = lows[1]

    pair_start(order[0], 2)
    pair_start(order[1])

    owned[t] = summed[t]

    down_spread = jnp.where(tenant_hit, down_low[None], 0.0).reshape(tenants * lowrank, tokens)
    adapted[...] = jnp.dot(
        jnp.transpose(down_spread).astype(jnp.bfloat16),
        up_ref[...].reshape(tenants * lowrank, w),
        preferred_element_type=jnp.float32,
    )
    for i, z in enumerate(order):
        part[z] = frozen(line + i)

    def up_copy(z, c):
        return pltpu.make_async_remote_copy(
            src_ref=part.at[z, rows_of(c)],
            dst_ref=going_up.at[z, rows_of(c)],
            send_sem=z_s.at[0],
            recv_sem=z_r.at[z * CHUNKS + c],
            device_id={"tensor": lax.rem(t + 2, n)},
            device_id_type=MESH,
        )

    def down_copy(z, c, last=False):
        slot_at = line if last else z
        return pltpu.make_async_remote_copy(
            src_ref=part.at[z, rows_of(c)],
            dst_ref=going_down.at[z, rows_of(c)],
            send_sem=z_s.at[0],
            recv_sem=z_r.at[slot_at * CHUNKS + c],
            device_id={"tensor": lax.rem(t + n - 2, n)},
            device_id_type=MESH,
        )

    def send_down(z, c):
        @pl.when(z == zi - 1)
        def _():
            down_copy(z, c, True).start()

        @pl.when(z < zi - 1)
        def _():
            down_copy(z, c).start()

    def pair_add(z, c):
        at = rows_of(c)
        pair_copy(z, c).wait_recv()
        part[z, at] = part[z, at] + yrecv[z, at]

    def ends(z, c):
        @pl.when(jnp.logical_and(zi == 0, z > 0))
        def _():
            up_copy(z, c).start()

        @pl.when(jnp.logical_and(zi == line - 1, z < line - 1))
        def _():
            send_down(z, c)

    def middles(z, c):
        at = rows_of(c)

        @pl.when(jnp.logical_and(zi > 0, zi < z))
        def _():
            up_copy(z, c).wait_recv()
            part[z, at] = part[z, at] + going_up[z, at]
            up_copy(z, c).start()

        @pl.when(jnp.logical_and(zi > z, zi < line - 1))
        def _():
            down_copy(z, c).wait_recv()
            part[z, at] = part[z, at] + going_down[z, at]
            send_down(z, c)

    for c in range(CHUNKS):
        pair_add(order[0], c)
        ends(order[0], c)
    for c in range(EARLY):
        middles(order[0], c)

    sent(state, msem.at[0])

    sent(owned.at[pl.ds(0, n - 1)], a_r.at[0])

    def squares_of(k, acc):
        g = owned[k]
        return acc + jnp.sum(g * g, axis=0)

    squares = lax.fori_loop(0, n, squares_of, jnp.zeros((lowrank, w), jnp.float32))
    squares = jnp.sum(squares, axis=(0, 1), keepdims=True)
    factor = clip_norm / jnp.maximum(jnp.sqrt(squares), clip_norm)

    def change_copy(o, source):
        return pltpu.make_async_remote_copy(
            src_ref=change.at[peer(o)],
            dst_ref=changes.at[source * 2 + d],
            send_sem=c_s.at[0],
            recv_sem=c_r.at[source],
            device_id={"tensor": peer(o)},
            device_id_type=MESH,
        )

    def half_copy(source):
        return pltpu.make_async_remote_copy(
            src_ref=change.at[lent_to, 1],
            dst_ref=changes.at[source * 2 + d, 1],
            send_sem=h_s.at[0],
            recv_sem=c_r.at[source],
            device_id={"tensor": lent_to},
            device_id_type=MESH,
        )

    scale_copy = pltpu.make_async_remote_copy(
        src_ref=scale_out,
        dst_ref=scale_in.at[lent_way],
        send_sem=h_s.at[1],
        recv_sem=s_r.at[lent_way],
        device_id={"tensor": lent_to},
        device_id_type=MESH,
    )
    scale_out[...] = jnp.broadcast_to(factor, scale_out.shape)
    scale_copy.start()

    def change_start(o):
        @pl.when(peer(o) != lent_to)
        def _():
            change_copy(o, t).start()

        @pl.when(peer(o) == lent_to)
        def _():
            half_copy(t).start()

    def step_piece(k):
        at = columns(k)
        for i in range(2):
            mean, power, moved = adam_step(
                owned[k, i], factor, state[i, 0, :, at], state[2 + i, 0, :, at]
            )
            state[i, 0, :, at] = mean
            state[2 + i, 0, :, at] = power
            change[k, i] = moved

    @pl.loop(1, n)
    def _(o):
        step_piece(peer(o))

        @pl.when(o > 1)
        def _():
            change_start(o - 1)

    step_piece(t)
    change_start(n - 1)
    changes[t * 2 + d] = change[t]

    for z in order[2:]:
        pair_start(z)

    def forward_copy(source, side):
        at = source * 2 + side
        return pltpu.make_async_remote_copy(
            src_ref=changes.at[at],
            dst_ref=changes.at[at],
            send_sem=f_s.at[0],
            recv_sem=f_r.at[0],
            device_id=mate,
            device_id_type=MESH,
        )

    forward_copy(t, d).start()
    state_outs = [
        pltpu.make_async_copy(state.at[i], ref, msem.at[0])
        for i, ref in enumerate((mean_down_ref, mean_up_ref, power_down_ref, power_up_ref))
    ]
    for copy in state_outs:
        copy.start()

    inner = jnp.logical_and(zi > 0, zi < line - 1)

    @pl.when(inner)
    def _():
        for c in range(EARLY, CHUNKS):
            middles(order[0], c)
        for k, c in INNER:
            pair_add(order[k], c)
            middles(order[k], c)

    @pl.when(jnp.logical_not(inner))
    def _():
        for k in (1, 2):
            for c in range(CHUNKS):
                pair_add(order[k], c)
                ends(order[k], c)

    for z in order[3:-1]:
        for c in range(CHUNKS):
            pair_add(z, c)
            ends(z, c)
            middles(z, c)

    @pl.loop(1, n)
    def _(o):
        source = giver(o)
        below = jnp.logical_and(from_below, source == t - 2)
        above = jnp.logical_and(from_above, source == t + 2)
        borrowed = jnp.logical_or(below, above)

        @pl.when(jnp.logical_not(borrowed))
        def _():
            change_copy(o, source).wait_recv()

        @pl.when(borrowed)
        def _():
            way = jnp.where(below, 0, 1)
            half_copy(source).wait_recv()
            sent(scale_in.at[way], s_r.at[way])
            sent(lent.at[way], l_r.at[way])
            scale = scale_in[way]
            changes[source * 2 + d, 0] = adam_step(
                summed[source, 0], scale[:1, :1], lent[way, 0], lent[way, 1]
            )[2]

        forward_copy(source, d).start()

    sent(changes.at[pl.ds(0, n)], f_r.at[0])

    @pl.loop(0, tenants)
    def _(k):
        back = changes[owner_ref[k]]
        new_down_ref[k] = (down_ref[k].astype(jnp.float32) - back[0]).astype(jnp.bfloat16)
        new_up_ref[k] = (up_ref[k].astype(jnp.float32) - back[1]).astype(jnp.bfloat16)

    adapter_outs = [
        pltpu.make_async_copy(new_down_ref, new_down_hbm, osem.at[0]),
        pltpu.make_async_copy(new_up_ref, new_up_hbm, osem.at[1]),
    ]
    for copy in adapter_outs:
        copy.start()

    def proj_out(c):
        at = rows_of(c)
        return pltpu.make_async_copy(proj_ref.at[at], proj_hbm.at[at], osem.at[2])

    for c in range(CHUNKS):
        at = rows_of(c)
        pair_add(zi, c)

        @pl.when(zi > 0)
        def _():
            up_copy(zi, c).wait_recv()
            part[zi, at] = part[zi, at] + going_up[zi, at]

        @pl.when(zi < line - 1)
        def _():
            down_copy(zi, c, True).wait_recv()
            part[zi, at] = part[zi, at] + going_down[zi, at]

        proj_ref[at] = (part[zi, at] + adapted[at]).astype(proj_ref.dtype)
        proj_out(c).start()

    sent(state, msem.at[0])
    for copy in adapter_outs:
        copy.wait()

    sent(rbuf.at[:, pl.ds(0, n - 1)], rank_s.at[0])
    tenant_copy.wait_send()
    sent(raw_out, g_s.at[1])
    for copy in low_copies:
        copy.wait_send()
    sent(change.at[pl.ds(0, n - 1)], a_s.at[0])
    sent(change.at[pl.ds(0, n - 2)], c_s.at[0])
    sent(change.at[0, 0], h_s.at[0])
    sent(scale_out, h_s.at[1])
    sent(lent.at[0], l_s.at[0])
    sent(changes.at[pl.ds(0, n)], f_s.at[0])
    sent(ysend, y_s.at[0])
    sent(part.at[pl.ds(0, line - 1)], z_s.at[0])
    sent(proj_ref, osem.at[2])


def hand_out(*refs):
    count = len(refs) // 2
    sems = refs[-1]
    outs = [pltpu.make_async_copy(refs[i], refs[count + i], sems.at[i]) for i in range(count)]
    for copy in outs:
        copy.start()
    for copy in outs:
        copy.wait()


def on_device(n, *args):
    (
        features,
        cotangent,
        token_tenant,
        owner_device,
        frozen_weight,
        adapter_down,
        adapter_up,
        momentum_down,
        momentum_up,
        variance_down,
        variance_up,
    ) = args
    tokens, depth = features.shape
    tenants, lowrank, w = adapter_down.shape
    line = n // 2
    f32 = jnp.float32
    bf16 = jnp.bfloat16
    hbm = pl.BlockSpec(memory_space=pltpu.HBM)
    anywhere = pl.BlockSpec(memory_space=pl.ANY)
    dma = pltpu.SemaphoreType.DMA
    shape = jax.ShapeDtypeStruct
    results = pl.pallas_call(
        functools.partial(kernel, n),
        out_shape=(
            shape((tokens, w), jnp.bfloat16),
            shape(adapter_down.shape, jnp.bfloat16),
            shape(adapter_up.shape, jnp.bfloat16),
            shape(momentum_down.shape, f32),
            shape(momentum_up.shape, f32),
            shape(variance_down.shape, f32),
            shape(variance_up.shape, f32),
        ),
        in_specs=[hbm] * 11,
        out_specs=[anywhere] * 7,
        scratch_shapes=[
            pltpu.SMEM((tenants,), jnp.int32),
            pltpu.VMEM((1, tokens), jnp.int32),
            pltpu.VMEM((1, tokens), jnp.int32),
            pltpu.VMEM((2, 2 * tokens, w), bf16),
            pltpu.VMEM(adapter_down.shape, bf16),
            pltpu.VMEM(adapter_up.shape, bf16),
            pltpu.VMEM((tokens, w), bf16),
            pltpu.VMEM(adapter_down.shape, bf16),
            pltpu.VMEM(adapter_up.shape, bf16),
            pltpu.VMEM((n, depth, w), jnp.bfloat16),
            pltpu.VMEM((4,) + momentum_down.shape, f32),
            pltpu.VMEM((2, lowrank, tokens), f32),
            pltpu.VMEM((2, n, lowrank, tokens), f32),
            pltpu.VMEM((2, tokens, w), f32),
            pltpu.VMEM((2, tokens, w), f32),
            pltpu.VMEM((2, lowrank, tokens), f32),
            pltpu.VMEM((2, lowrank, tokens), f32),
            pltpu.VMEM((n, 2, lowrank, w), f32),
            pltpu.VMEM((n, 2, lowrank, w), f32),
            pltpu.VMEM((n, 2, lowrank, w), f32),
            pltpu.VMEM((tenants, 2, lowrank, w), f32),
            pltpu.VMEM((line, tokens, w), f32),
            pltpu.VMEM((line, tokens, w), f32),
            pltpu.VMEM((line, tokens, w), f32),
            pltpu.VMEM((line, tokens, w), f32),
            pltpu.VMEM((line, tokens, w), f32),
            pltpu.VMEM((tokens, w), f32),
            pltpu.VMEM((2, 2, lowrank, w), f32),
            pltpu.VMEM((8, 128), f32),
            pltpu.VMEM((2, 8, 128), f32),
            dma((6,)),
            dma((3,)),
            dma((n,)),
            dma((1,)),
            dma((1,)),
            dma((2,)),
            dma((4,)),
            dma((5,)),
            dma((1,)),
            dma((1,)),
            dma((1,)),
            dma((n,)),
            dma((1,)),
            dma((1,)),
            dma((1,)),
            dma((line * CHUNKS,)),
            dma((1,)),
            dma(((line + 1) * CHUNKS,)),
            dma((1,)),
            dma((2,)),
            dma((2,)),
            dma((2,)),
        ],
        compiler_params=pltpu.CompilerParams(
            collective_id=0, has_side_effects=True, vmem_limit_bytes=48 * 1024 * 1024
        ),
    )(
        *(
            pltpu.with_memory_space_constraint(x, pltpu.HBM)
            for x in (
                owner_device,
                token_tenant.reshape(1, tokens),
                features,
                cotangent,
                adapter_down,
                adapter_up,
                frozen_weight,
                momentum_down,
                momentum_up,
                variance_down,
                variance_up,
            )
        )
    )
    return pl.pallas_call(
        hand_out,
        out_shape=tuple(shape(r.shape, r.dtype) for r in results),
        in_specs=[anywhere] * len(results),
        out_specs=[hbm] * len(results),
        scratch_shapes=[dma((len(results),))],
        compiler_params=pltpu.CompilerParams(vmem_limit_bytes=1024 * 1024),
    )(*results)


def solution(mesh):
    in_specs = (
        P(("group", "dp"), "tensor"),
        P(("group", "dp"), "tensor"),
        P(("group", "dp")),
        P("group"),
        P("tensor", None),
        P("group", None, "tensor"),
        P("group", None, "tensor"),
        P(("group", "tensor", "dp"), None, None),
        P(("group", "tensor", "dp"), None, None),
        P(("group", "tensor", "dp"), None, None),
        P(("group", "tensor", "dp"), None, None),
    )
    out_specs = (
        P(("group", "dp"), "tensor"),
        P("group", None, "tensor"),
        P("group", None, "tensor"),
        P(("group", "tensor", "dp"), None, None),
        P(("group", "tensor", "dp"), None, None),
        P(("group", "tensor", "dp"), None, None),
        P(("group", "tensor", "dp"), None, None),
    )
    return jax.shard_map(
        functools.partial(on_device, mesh.shape["tensor"]),
        mesh=mesh,
        in_specs=in_specs,
        out_specs=out_specs,
        check_vma=False,
    )
```

```python
import functools

import jax
import jax.numpy as jnp
from jax import lax
from jax.experimental import pallas as pl
from jax.experimental.pallas import tpu as pltpu
from jax.sharding import PartitionSpec as P

MESH = pl.DeviceIdType.MESH

adapter_scale = 2.0
clip_norm = 12000.0
learn_rate = 0.004
beta_one = 0.9
beta_two = 0.999
adam_eps = 1e-08
correct_one = 1.0 - beta_one**20
correct_two = 1.0 - beta_two**20

CHUNKS = 4
EARLY = 1
LEND_AT = 0
INNER = ((1, 0), (1, 1), (2, 0), (2, 1), (1, 2), (2, 2), (1, 3), (2, 3))


def adam_step(gradient, factor, moment, square):
    clipped = gradient * factor
    moment_next = beta_one * moment + (1.0 - beta_one) * clipped
    square_next = beta_two * square + (1.0 - beta_two) * clipped * clipped
    change = (
        learn_rate * (moment_next / correct_one) / (jnp.sqrt(square_next / correct_two) + adam_eps)
    )
    return (moment_next, square_next, change)


def block_order(line, zi):
    low = zi < line // 2
    near = jnp.where(low, zi, line - 1 - zi)
    order = []
    for k in range(line - 1):
        far_first = line - 1 - (k // 2 if k % 2 == 0 else k // 2)
        paired = far_first if k % 2 == 0 else k // 2
        alone = line - 1 - (k - near)
        place = jnp.where(k < 2 * near, paired, alone)
        order.append(jnp.where(low, place, line - 1 - place))
    order.append(zi)
    return order


def kernel(
    n,
    owner_hbm,
    tenant_hbm,
    feat_hbm,
    cot_hbm,
    down_hbm,
    up_hbm,
    weight_ref,
    mom_down_ref,
    mom_up_ref,
    var_down_ref,
    var_up_ref,
    proj_hbm,
    new_down_hbm,
    new_up_hbm,
    mean_down_ref,
    mean_up_ref,
    power_down_ref,
    power_up_ref,
    owner_ref,
    tenant_ref,
    mate_tenant,
    rows_ref,
    down_ref,
    up_ref,
    proj_ref,
    new_down_ref,
    new_up_ref,
    wbuf,
    state,
    rpart,
    rbuf,
    raw_out,
    raw_in,
    low_out,
    low_in,
    summed,
    owned,
    change,
    changes,
    ysend,
    yrecv,
    part,
    going_up,
    going_down,
    adapted,
    lent,
    scale_out,
    scale_in,
    isem,
    osem,
    wsem,
    msem,
    rank_s,
    rank_r,
    g_s,
    g_r,
    a_s,
    a_r,
    c_s,
    c_r,
    f_s,
    f_r,
    y_s,
    y_r,
    z_s,
    z_r,
    l_s,
    l_r,
    h_s,
    s_r,
):
    tenants, lowrank, w = down_ref.shape
    tokens = tenant_ref.shape[1]
    feat_ref, cot_ref = (rows_ref.at[i, pl.ds(0, tokens)] for i in range(2))
    line = n // 2
    t = lax.axis_index("tensor")
    d = lax.axis_index("dp")
    zi, yi = t // 2, lax.rem(t, 2)
    mate = {"dp": 1 - d}
    pair = {"tensor": zi * 2 + 1 - yi}
    order = block_order(line, zi)
    height = tokens // CHUNKS
    low_side = zi < line // 2
    lent_to = jnp.where(low_side, t + 2, t - 2)
    lent_way = jnp.where(low_side, 0, 1)
    from_below = jnp.logical_and(zi > 0, zi - 1 < line // 2)
    from_above = jnp.logical_and(zi < line - 1, zi + 1 >= line // 2)
    paired = n & (n - 1) == 0

    def peer(o):
        return t ^ (n - o) if paired else lax.rem(t + o, n)

    def giver(o):
        return t ^ (n - o) if paired else lax.rem(t + n - o, n)

    def columns(block):
        return pl.ds(pl.multiple_of(block * w, w), w)

    def sent(ref, sem):
        pltpu.make_async_copy(ref, ref, sem).wait()

    barrier = pltpu.get_barrier_semaphore()

    in_copies = [
        pltpu.make_async_copy(src, dst, isem.at[i])
        for i, (src, dst) in enumerate(
            (
                (tenant_hbm, tenant_ref),
                (cot_hbm, cot_ref),
                (up_hbm, up_ref),
                (feat_hbm, feat_ref),
                (down_hbm, down_ref),
                (owner_hbm, owner_ref),
            )
        )
    ]
    for copy in in_copies:
        copy.start()

    @pl.loop(1, n)
    def _(o):
        pl.semaphore_signal(barrier, inc=1, device_id={"tensor": peer(o)}, device_id_type=MESH)

    pl.semaphore_signal(barrier, inc=1, device_id=mate, device_id_type=MESH)

    def weight_copy(i, block):
        return pltpu.make_async_copy(
            weight_ref.at[:, columns(block)], wbuf.at[i], wsem.at[i]
        )

    blocks = [z * 2 + 1 - yi for z in order] + [z * 2 + yi for z in order]
    in_copies[0].wait()
    tenant = tenant_ref[...]
    contract = (((1,), (1,)), ((), ()))
    tenant_row = lax.broadcasted_iota(jnp.int32, (tenants, lowrank, tokens), 0)
    tenant_hit = tenant_row == tenant[None]

    def rank_part(adapter, rows):
        scores = lax.dot_general(
            adapter[...].reshape(tenants * lowrank, w),
            rows[...],
            contract,
            preferred_element_type=jnp.float32,
        ).reshape(tenants, lowrank, tokens)
        return jnp.sum(jnp.where(tenant_hit, scores, 0.0), axis=0)

    for copy in in_copies[1:3]:
        copy.wait()
    rpart[0] = rank_part(up_ref, cot_ref)
    for copy in in_copies[3:]:
        copy.wait()
    for i, block in enumerate(blocks):
        weight_copy(i, block).start()
    state_copies = [
        pltpu.make_async_copy(ref, state.at[i], msem.at[0])
        for i, ref in enumerate((mom_down_ref, mom_up_ref, var_down_ref, var_up_ref))
    ]
    for copy in state_copies:
        copy.start()
    pl.semaphore_wait(barrier, n)

    def rank_copy(o, source, side):
        return pltpu.make_async_remote_copy(
            src_ref=rpart.at[side],
            dst_ref=rbuf.at[side, source],
            send_sem=rank_s.at[0],
            recv_sem=rank_r.at[side],
            device_id={"tensor": peer(o)},
            device_id_type=MESH,
        )

    @pl.loop(1, n)
    def _(o):
        rank_copy(o, t, 0).start()

    rpart[1] = rank_part(down_ref, feat_ref)

    @pl.loop(1, n)
    def _(o):
        rank_copy(o, t, 1).start()

    def mate_copy(source, target, out, arrived):
        return pltpu.make_async_remote_copy(
            src_ref=source,
            dst_ref=target,
            send_sem=g_s.at[out],
            recv_sem=g_r.at[arrived],
            device_id=mate,
            device_id_type=MESH,
        )

    tenant_copy = mate_copy(tenant_ref, mate_tenant, 0, 0)
    raw_copies = [mate_copy(raw_out.at[i], raw_in.at[i], 1, 1 + i) for i in range(2)]
    low_copies = [mate_copy(low_out.at[i], low_in.at[i], 2 + i, 3 + i) for i in range(2)]
    tenant_copy.start()
    for i, rows in enumerate((feat_ref, cot_ref)):
        raw_out[i] = rows[...].astype(jnp.float32)
        raw_copies[i].start()

    def lent_copy(i):
        return pltpu.make_async_remote_copy(
            src_ref=(mom_down_ref, var_down_ref)[i].at[0, :, columns(lent_to)],
            dst_ref=lent.at[lent_way, i],
            send_sem=l_s.at[0],
            recv_sem=l_r.at[lent_way],
            device_id={"tensor": lent_to},
            device_id_type=MESH,
        )

    def rows_of(c):
        return pl.ds(c * height, height)

    def pair_copy(z, c):
        return pltpu.make_async_remote_copy(
            src_ref=ysend.at[z, rows_of(c)],
            dst_ref=yrecv.at[z, rows_of(c)],
            send_sem=y_s.at[0],
            recv_sem=y_r.at[z * CHUNKS + c],
            device_id=pair,
            device_id_type=MESH,
        )

    def pair_start(z, first=0, last=CHUNKS):
        for c in range(first, last):
            pair_copy(z, c).start()

    def frozen(i):
        sent(wbuf.at[i], wsem.at[i])
        return jnp.dot(feat_ref[...], wbuf[i], preferred_element_type=jnp.float32)

    for i, z in enumerate(order):
        ysend[z] = frozen(i)
        if i == 0:
            pair_start(z, 0, 2)
        if i == LEND_AT:
            for k in range(2):
                lent_copy(k).start()

    tenant_copy.wait_recv()
    tenants_here = (tenant, mate_tenant[...])
    slots = lax.fori_loop(
        0,
        tenants,
        lambda k, found: tuple(
            jnp.where(here == k, owner_ref[k], s) for here, s in zip(tenants_here, found)
        ),
        tuple(jnp.zeros_like(here) for here in tenants_here),
    )
    for i in range(2):
        raw_copies[i].wait_recv()
        rows_ref[i, tokens:] = raw_in[i].astype(jnp.bfloat16)

    half_row = lax.broadcasted_iota(jnp.int32, (n, lowrank, tokens), 0) * 2 + d

    def spread(values, slot):
        picked = jnp.where(half_row == slot[None], values[None], 0.0)
        return picked.reshape(n * lowrank, tokens).astype(jnp.bfloat16)

    def grad_copy(o, source, side):
        return pltpu.make_async_remote_copy(
            src_ref=summed.at[peer(o), side],
            dst_ref=owned.at[source, side],
            send_sem=a_s.at[0],
            recv_sem=a_r.at[0],
            device_id={"tensor": peer(o)},
            device_id_type=MESH,
        )

    lows = []
    for i in range(2):
        sent(rbuf.at[i, pl.ds(0, n - 1)], rank_r.at[i])
        rbuf[i, t] = rpart[i]
        total = rbuf[i, 0]
        for source in range(1, n):
            total = total + rbuf[i, source]
        low = (adapter_scale * total).astype(jnp.bfloat16).astype(jnp.float32)
        low_out[i] = low
        low_copies[i].start()
        own_part = spread(low, slots[0])
        lows.append(low)
        low_copies[i].wait_recv()
        summed[:, i] = jnp.dot(
            jnp.concatenate([own_part, spread(low_in[i], slots[1])], axis=1),
            rows_ref[i],
            preferred_element_type=jnp.float32,
        ).reshape(n, lowrank, w)

        @pl.loop(1, n)
        def _(o):
            grad_copy(o, t, i).start()

    down_low = lows[1]

    pair_start(order[0], 2)
    pair_start(order[1])

    owned[t] = summed[t]

    down_spread = jnp.where(tenant_hit, down_low[None], 0.0).reshape(tenants * lowrank, tokens)
    adapted[...] = jnp.dot(
        jnp.transpose(down_spread).astype(jnp.bfloat16),
        up_ref[...].reshape(tenants * lowrank, w),
        preferred_element_type=jnp.float32,
    )
    for i, z in enumerate(order):
        part[z] = frozen(line + i)

    def up_copy(z, c):
        return pltpu.make_async_remote_copy(
            src_ref=part.at[z, rows_of(c)],
            dst_ref=going_up.at[z, rows_of(c)],
            send_sem=z_s.at[0],
            recv_sem=z_r.at[z * CHUNKS + c],
            device_id={"tensor": lax.rem(t + 2, n)},
            device_id_type=MESH,
        )

    def down_copy(z, c, last=False):
        slot_at = line if last else z
        return pltpu.make_async_remote_copy(
            src_ref=part.at[z, rows_of(c)],
            dst_ref=going_down.at[z, rows_of(c)],
            send_sem=z_s.at[0],
            recv_sem=z_r.at[slot_at * CHUNKS + c],
            device_id={"tensor": lax.rem(t + n - 2, n)},
            device_id_type=MESH,
        )

    def send_down(z, c):
        @pl.when(z == zi - 1)
        def _():
            down_copy(z, c, True).start()

        @pl.when(z < zi - 1)
        def _():
            down_copy(z, c).start()

    def pair_add(z, c):
        at = rows_of(c)
        pair_copy(z, c).wait_recv()
        part[z, at] = part[z, at] + yrecv[z, at]

    def ends(z, c):
        @pl.when(jnp.logical_and(zi == 0, z > 0))
        def _():
            up_copy(z, c).start()

        @pl.when(jnp.logical_and(zi == line - 1, z < line - 1))
        def _():
            send_down(z, c)

    def middles(z, c):
        at = rows_of(c)

        @pl.when(jnp.logical_and(zi > 0, zi < z))
        def _():
            up_copy(z, c).wait_recv()
            part[z, at] = part[z, at] + going_up[z, at]
            up_copy(z, c).start()

        @pl.when(jnp.logical_and(zi > z, zi < line - 1))
        def _():
            down_copy(z, c).wait_recv()
            part[z, at] = part[z, at] + going_down[z, at]
            send_down(z, c)

    for c in range(CHUNKS):
        pair_add(order[0], c)
        ends(order[0], c)
    for c in range(EARLY):
        middles(order[0], c)

    sent(state, msem.at[0])

    sent(owned.at[pl.ds(0, n - 1)], a_r.at[0])

    def squares_of(k, acc):
        g = owned[k]
        return acc + jnp.sum(g * g, axis=0)

    squares = lax.fori_loop(0, n, squares_of, jnp.zeros((lowrank, w), jnp.float32))
    squares = jnp.sum(squares, axis=(0, 1), keepdims=True)
    factor = clip_norm / jnp.maximum(jnp.sqrt(squares), clip_norm)

    def change_copy(o, source):
        return pltpu.make_async_remote_copy(
            src_ref=change.at[peer(o)],
            dst_ref=changes.at[source * 2 + d],
            send_sem=c_s.at[0],
            recv_sem=c_r.at[source],
            device_id={"tensor": peer(o)},
            device_id_type=MESH,
        )

    def half_copy(source):
        return pltpu.make_async_remote_copy(
            src_ref=change.at[lent_to, 1],
            dst_ref=changes.at[source * 2 + d, 1],
            send_sem=h_s.at[0],
            recv_sem=c_r.at[source],
            device_id={"tensor": lent_to},
            device_id_type=MESH,
        )

    scale_copy = pltpu.make_async_remote_copy(
        src_ref=scale_out,
        dst_ref=scale_in.at[lent_way],
        send_sem=h_s.at[1],
        recv_sem=s_r.at[lent_way],
        device_id={"tensor": lent_to},
        device_id_type=MESH,
    )
    scale_out[...] = jnp.broadcast_to(factor, scale_out.shape)
    scale_copy.start()

    def change_start(o):
        @pl.when(peer(o) != lent_to)
        def _():
            change_copy(o, t).start()

        @pl.when(peer(o) == lent_to)
        def _():
            half_copy(t).start()

    def step_piece(k):
        at = columns(k)
        for i in range(2):
            mean, power, moved = adam_step(
                owned[k, i], factor, state[i, 0, :, at], state[2 + i, 0, :, at]
            )
            state[i, 0, :, at] = mean
            state[2 + i, 0, :, at] = power
            change[k, i] = moved

    @pl.loop(1, n)
    def _(o):
        step_piece(peer(o))

        @pl.when(o > 1)
        def _():
            change_start(o - 1)

    step_piece(t)
    change_start(n - 1)
    changes[t * 2 + d] = change[t]

    for z in order[2:]:
        pair_start(z)

    def forward_copy(source, side):
        at = source * 2 + side
        return pltpu.make_async_remote_copy(
            src_ref=changes.at[at],
            dst_ref=changes.at[at],
            send_sem=f_s.at[0],
            recv_sem=f_r.at[0],
            device_id=mate,
            device_id_type=MESH,
        )

    forward_copy(t, d).start()
    state_outs = [
        pltpu.make_async_copy(state.at[i], ref, msem.at[0])
        for i, ref in enumerate((mean_down_ref, mean_up_ref, power_down_ref, power_up_ref))
    ]
    for copy in state_outs:
        copy.start()

    inner = jnp.logical_and(zi > 0, zi < line - 1)

    @pl.when(inner)
    def _():
        for c in range(EARLY, CHUNKS):
            middles(order[0], c)
        for k, c in INNER:
            pair_add(order[k], c)
            middles(order[k], c)

    @pl.when(jnp.logical_not(inner))
    def _():
        for k in (1, 2):
            for c in range(CHUNKS):
                pair_add(order[k], c)
                ends(order[k], c)

    for z in order[3:-1]:
        for c in range(CHUNKS):
            pair_add(z, c)
            ends(z, c)
            middles(z, c)

    @pl.loop(1, n)
    def _(o):
        source = giver(o)
        below = jnp.logical_and(from_below, source == t - 2)
        above = jnp.logical_and(from_above, source == t + 2)
        borrowed = jnp.logical_or(below, above)

        @pl.when(jnp.logical_not(borrowed))
        def _():
            change_copy(o, source).wait_recv()

        @pl.when(borrowed)
        def _():
            way = jnp.where(below, 0, 1)
            half_copy(source).wait_recv()
            sent(scale_in.at[way], s_r.at[way])
            sent(lent.at[way], l_r.at[way])
            scale = scale_in[way]
            changes[source * 2 + d, 0] = adam_step(
                summed[source, 0], scale[:1, :1], lent[way, 0], lent[way, 1]
            )[2]

        forward_copy(source, d).start()

    sent(changes.at[pl.ds(0, n)], f_r.at[0])

    @pl.loop(0, tenants)
    def _(k):
        back = changes[owner_ref[k]]
        new_down_ref[k] = (down_ref[k].astype(jnp.float32) - back[0]).astype(jnp.bfloat16)
        new_up_ref[k] = (up_ref[k].astype(jnp.float32) - back[1]).astype(jnp.bfloat16)

    adapter_outs = [
        pltpu.make_async_copy(new_down_ref, new_down_hbm, osem.at[0]),
        pltpu.make_async_copy(new_up_ref, new_up_hbm, osem.at[1]),
    ]
    for copy in adapter_outs:
        copy.start()

    def proj_out(c):
        at = rows_of(c)
        return pltpu.make_async_copy(proj_ref.at[at], proj_hbm.at[at], osem.at[2])

    for c in range(CHUNKS):
        at = rows_of(c)
        pair_add(zi, c)

        @pl.when(zi > 0)
        def _():
            up_copy(zi, c).wait_recv()
            part[zi, at] = part[zi, at] + going_up[zi, at]

        @pl.when(zi < line - 1)
        def _():
            down_copy(zi, c, True).wait_recv()
            part[zi, at] = part[zi, at] + going_down[zi, at]

        proj_ref[at] = (part[zi, at] + adapted[at]).astype(proj_ref.dtype)
        proj_out(c).start()

    sent(state, msem.at[0])
    for copy in adapter_outs:
        copy.wait()

    sent(rbuf.at[:, pl.ds(0, n - 1)], rank_s.at[0])
    tenant_copy.wait_send()
    sent(raw_out, g_s.at[1])
    for copy in low_copies:
        copy.wait_send()
    sent(change.at[pl.ds(0, n - 1)], a_s.at[0])
    sent(change.at[pl.ds(0, n - 2)], c_s.at[0])
    sent(change.at[0, 0], h_s.at[0])
    sent(scale_out, h_s.at[1])
    sent(lent.at[0], l_s.at[0])
    sent(changes.at[pl.ds(0, n)], f_s.at[0])
    sent(ysend, y_s.at[0])
    sent(part.at[pl.ds(0, line - 1)], z_s.at[0])
    sent(proj_ref, osem.at[2])


def hand_out(*refs):
    count = len(refs) // 2
    sems = refs[-1]
    outs = [pltpu.make_async_copy(refs[i], refs[count + i], sems.at[i]) for i in range(count)]
    for copy in outs:
        copy.start()
    for copy in outs:
        copy.wait()


def on_device(n, *args):
    (
        features,
        cotangent,
        token_tenant,
        owner_device,
        frozen_weight,
        adapter_down,
        adapter_up,
        momentum_down,
        momentum_up,
        variance_down,
        variance_up,
    ) = args
    tokens, depth = features.shape
    tenants, lowrank, w = adapter_down.shape
    line = n // 2
    f32 = jnp.float32
    bf16 = jnp.bfloat16
    hbm = pl.BlockSpec(memory_space=pltpu.HBM)
    anywhere = pl.BlockSpec(memory_space=pl.ANY)
    dma = pltpu.SemaphoreType.DMA
    shape = jax.ShapeDtypeStruct
    results = pl.pallas_call(
        functools.partial(kernel, n),
        out_shape=(
            shape((tokens, w), jnp.bfloat16),
            shape(adapter_down.shape, jnp.bfloat16),
            shape(adapter_up.shape, jnp.bfloat16),
            shape(momentum_down.shape, f32),
            shape(momentum_up.shape, f32),
            shape(variance_down.shape, f32),
            shape(variance_up.shape, f32),
        ),
        in_specs=[hbm] * 11,
        out_specs=[anywhere] * 7,
        scratch_shapes=[
            pltpu.SMEM((tenants,), jnp.int32),
            pltpu.VMEM((1, tokens), jnp.int32),
            pltpu.VMEM((1, tokens), jnp.int32),
            pltpu.VMEM((2, 2 * tokens, w), bf16),
            pltpu.VMEM(adapter_down.shape, bf16),
            pltpu.VMEM(adapter_up.shape, bf16),
            pltpu.VMEM((tokens, w), bf16),
            pltpu.VMEM(adapter_down.shape, bf16),
            pltpu.VMEM(adapter_up.shape, bf16),
            pltpu.VMEM((n, depth, w), jnp.bfloat16),
            pltpu.VMEM((4,) + momentum_down.shape, f32),
            pltpu.VMEM((2, lowrank, tokens), f32),
            pltpu.VMEM((2, n, lowrank, tokens), f32),
            pltpu.VMEM((2, tokens, w), f32),
            pltpu.VMEM((2, tokens, w), f32),
            pltpu.VMEM((2, lowrank, tokens), f32),
            pltpu.VMEM((2, lowrank, tokens), f32),
            pltpu.VMEM((n, 2, lowrank, w), f32),
            pltpu.VMEM((n, 2, lowrank, w), f32),
            pltpu.VMEM((n, 2, lowrank, w), f32),
            pltpu.VMEM((tenants, 2, lowrank, w), f32),
            pltpu.VMEM((line, tokens, w), f32),
            pltpu.VMEM((line, tokens, w), f32),
            pltpu.VMEM((line, tokens, w), f32),
            pltpu.VMEM((line, tokens, w), f32),
            pltpu.VMEM((line, tokens, w), f32),
            pltpu.VMEM((tokens, w), f32),
            pltpu.VMEM((2, 2, lowrank, w), f32),
            pltpu.VMEM((8, 128), f32),
            pltpu.VMEM((2, 8, 128), f32),
            dma((6,)),
            dma((3,)),
            dma((n,)),
            dma((1,)),
            dma((1,)),
            dma((2,)),
            dma((4,)),
            dma((5,)),
            dma((1,)),
            dma((1,)),
            dma((1,)),
            dma((n,)),
            dma((1,)),
            dma((1,)),
            dma((1,)),
            dma((line * CHUNKS,)),
            dma((1,)),
            dma(((line + 1) * CHUNKS,)),
            dma((1,)),
            dma((2,)),
            dma((2,)),
            dma((2,)),
        ],
        compiler_params=pltpu.CompilerParams(
            collective_id=0, has_side_effects=True, vmem_limit_bytes=48 * 1024 * 1024
        ),
    )(
        *(
            pltpu.with_memory_space_constraint(x, pltpu.HBM)
            for x in (
                owner_device,
                token_tenant.reshape(1, tokens),
                features,
                cotangent,
                adapter_down,
                adapter_up,
                frozen_weight,
                momentum_down,
                momentum_up,
                variance_down,
                variance_up,
            )
        )
    )
    return pl.pallas_call(
        hand_out,
        out_shape=tuple(shape(r.shape, r.dtype) for r in results),
        in_specs=[anywhere] * len(results),
        out_specs=[hbm] * len(results),
        scratch_shapes=[dma((len(results),))],
        compiler_params=pltpu.CompilerParams(vmem_limit_bytes=1024 * 1024),
    )(*results)


def solution(mesh):
    in_specs = (
        P(("group", "dp"), "tensor"),
        P(("group", "dp"), "tensor"),
        P(("group", "dp")),
        P("group"),
        P("tensor", None),
        P("group", None, "tensor"),
        P("group", None, "tensor"),
        P(("group", "tensor", "dp"), None, None),
        P(("group", "tensor", "dp"), None, None),
        P(("group", "tensor", "dp"), None, None),
        P(("group", "tensor", "dp"), None, None),
    )
    out_specs = (
        P(("group", "dp"), "tensor"),
        P("group", None, "tensor"),
        P("group", None, "tensor"),
        P(("group", "tensor", "dp"), None, None),
        P(("group", "tensor", "dp"), None, None),
        P(("group", "tensor", "dp"), None, None),
        P(("group", "tensor", "dp"), None, None),
    )
    return jax.shard_map(
        functools.partial(on_device, mesh.shape["tensor"]),
        mesh=mesh,
        in_specs=in_specs,
        out_specs=out_specs,
        check_vma=False,
    )
```
